32 devices in a mesh: frame: 8 (over z, y), row: 4 (over x, core).
Axes of the slice: x: 2, y: 2, z: 4, core: 2. Of those that a mesh axis runs over, the one named last changes fastest.
Arguments:
- queries: bfloat16 [8, 640, 2560], P('frame', 'row'), may hold values from -6 to 6
- keys: bfloat16 [8, 640, 2560], P('frame', 'row'), may hold values from -6 to 6
- values: bfloat16 [8, 640, 2560], P('frame', 'row'), may hold values from -6 to 6
- band: int32 [8, 5], P('frame'), may hold values from -1 to 1, as said below
Outputs:
- attended: bfloat16 [8, 640, 2560], P('frame', 'row')
The draws below stay inside these ranges and needn't reach their ends.
Inputs may be any that keep to these rules, and one draw needn't show every extreme that they name: band[f, 0] and band[f, 4] are -1 or 0; band[f, 1] and band[f, 3] are -1, 0 or 1; band[f, 2] is 0 or 1.
All inputs are finite; a program needn't handle non-finite values.
Results may differ from the reference program's by a relative error of at most 0.0033.
Values may be sent and summed in bfloat16 or wider, within the bound.
No kernel may reach another device: no remote copies, remote signals or barrier semaphores. Data moves between devices by JAX's collectives and lax.ppermute only.
A program may use at most 128 MiB of HBM per device.

```python
import jax
import jax.numpy as jnp
from jax import lax

HEADS = 20
HEAD = 128
ROWTOK = 160
FRAMES = 8
ROWS = 640
HD = 2560
N_ROW = 4


def draw_queries(key, part):
    shape = (FRAMES, ROWTOK * N_ROW, HEADS * HEAD)
    own_key = jax.random.fold_in(key, 1)
    return jnp.clip(1.5 * jax.random.normal(own_key, shape, jnp.float32), -6.0, 6.0).astype(jnp.bfloat16)


def draw_keys(key, part):
    shape = (FRAMES, ROWTOK * N_ROW, HEADS * HEAD)
    own_key = jax.random.fold_in(key, 2)
    return jnp.clip(1.5 * jax.random.normal(own_key, shape, jnp.float32), -6.0, 6.0).astype(jnp.bfloat16)


def draw_band(key, part):
    lowest = jnp.array([-1, -1, 0, -1, -1], dtype=jnp.int32)
    highest = jnp.array([0, 1, 1, 1, 0], dtype=jnp.int32)
    raw = jax.random.randint(jax.random.fold_in(key, 4), (FRAMES, 5), 0, 1 << 20)
    drawn = lowest[None, :] + raw % (highest - lowest + 1)[None, :]
    full_frame = jax.random.randint(jax.random.fold_in(key, 3), (), 0, FRAMES)
    sparse_frame = (full_frame + FRAMES // 2) % FRAMES
    frame_ids = jnp.arange(FRAMES, dtype=jnp.int32)[:, None]
    drawn = jnp.where(frame_ids == full_frame, highest[None, :], drawn)
    drawn = jnp.where(frame_ids == sparse_frame, lowest[None, :], drawn)
    return drawn.astype(jnp.int32)


def block_levels(stream_key, dims, shards, smallest, high):
    gain = 1.0
    for axis_at, blocks in shards:
        draws = jax.random.uniform(jax.random.fold_in(jax.random.fold_in(stream_key, 6), axis_at), (blocks,), jnp.float32, smallest / len(shards), high / len(shards))
        gain = gain * jnp.repeat(jnp.exp(draws), dims[axis_at] // blocks).reshape((-1,) + (1,) * (len(dims) - 1 - axis_at))
    return gain


def noise(key, dims, scale, bound, shards=(), kind=jnp.bfloat16):
    entries = scale * jax.random.normal(key, dims, jnp.float32)
    if shards:
        entries = entries * block_levels(key, dims, shards, -0.22, 0.18)
    return jnp.clip(entries, -bound, bound).astype(kind)


def setup_inputs(seed: int = 0) -> dict:
    arg_keys = jax.random.split(jax.random.key(seed), 5)
    return {
        "queries": draw_queries(jax.random.fold_in(arg_keys[4], 71), 0),
        "keys": draw_keys(jax.random.fold_in(arg_keys[4], 71), 0),
        "values": noise(arg_keys[2], (FRAMES, ROWS, HD), 1.0, 6.0, ((0, 8), (1, 4))),
        "band": draw_band(jax.random.fold_in(arg_keys[4], 71), 0),
    }


CANDIDATES = [(-2, 0)] + [(frame_step, band_step) for frame_step in (-1, 0, 1) for band_step in (-1, 0, 1)] + [(2, 0)]


def attend(query_tile, key_pieces, value_pieces, keep_mask):
    tile_rows = query_tile.shape[0]
    heads = query_tile.shape[1] // HEAD

    def one_head(head_index):
        start = (head_index * HEAD).astype(jnp.int32)
        q_head = lax.dynamic_slice_in_dim(query_tile, start, HEAD, 1)
        k_head = jnp.concatenate([lax.dynamic_slice_in_dim(piece, start, HEAD, 1) for piece in key_pieces], 0)
        v_head = jnp.concatenate([lax.dynamic_slice_in_dim(piece, start, HEAD, 1) for piece in value_pieces], 0)
        scores = jnp.dot(q_head, k_head.T, preferred_element_type=jnp.float32) * (HEAD ** -0.5)
        scores = jnp.where(keep_mask[None, :], scores, -jnp.inf)
        largest = jnp.max(scores, axis=1, keepdims=True)
        expo = jnp.exp(scores - largest)
        total = jnp.sum(expo, axis=1, keepdims=True)
        weights = expo.astype(jnp.bfloat16)
        return jnp.dot(weights, v_head, preferred_element_type=jnp.float32) / total

    result = lax.map(one_head, jnp.arange(heads, dtype=jnp.int32))
    return result.transpose(1, 0, 2).reshape(tile_rows, heads * HEAD).astype(jnp.bfloat16)


def reference(queries, keys, values, band):
    query_tiles = queries.reshape(FRAMES, N_ROW, ROWTOK, HEADS * HEAD)
    key_tiles = keys.reshape(FRAMES, N_ROW, ROWTOK, HEADS * HEAD)
    value_tiles = values.reshape(FRAMES, N_ROW, ROWTOK, HEADS * HEAD)
    bands_all = jnp.arange(N_ROW, dtype=jnp.int32)

    def per_frame(frame_index):
        key_pieces = []
        value_pieces = []
        keep_flags = []
        band_row = band[frame_index]
        for frame_step, band_step in CANDIDATES:
            source = ((frame_index + frame_step) % FRAMES).astype(jnp.int32)
            target = jnp.clip(bands_all + band_step, 0, N_ROW - 1).astype(jnp.int32)
            key_pieces.append(key_tiles[source][target])
            value_pieces.append(value_tiles[source][target])
            inside = (bands_all + band_step >= 0) & (bands_all + band_step < N_ROW)
            keep_flags.append(inside & (abs(band_step) <= band_row[frame_step + 2]))
        keep_mask = jnp.repeat(jnp.stack(keep_flags, axis=1), ROWTOK, axis=1)
        return jax.vmap(attend)(query_tiles[frame_index], key_pieces, value_pieces, keep_mask)

    result = lax.map(per_frame, jnp.arange(FRAMES, dtype=jnp.int32))
    return result.reshape(FRAMES, N_ROW * ROWTOK, HEADS * HEAD)
```

```python
import functools

import jax
import jax.numpy as jnp
from jax import lax
from jax.experimental import pallas as pl
from jax.experimental.pallas import tpu as pltpu
from jax.sharding import PartitionSpec as P


HEAD = 128
LANES = 128
GROUP = 5
NEG = -1e30


def scores_of(query, key):
    return lax.dot_general(
        query, key, (((1,), (1,)), ((), ())), preferred_element_type=jnp.float32
    ) * HEAD ** (-0.5)


def softmax_part(query, keys, values, keeps):
    scores = [
        jnp.where(keep, scores_of(query, key), NEG) for key, keep in zip(keys, keeps)
    ]
    largest = functools.reduce(
        jnp.maximum, [jnp.max(score, axis=1, keepdims=True) for score in scores]
    )
    total = 0.0
    summed = 0.0
    for score, value in zip(scores, values):
        expo = jnp.exp(score - largest)
        total = total + jnp.sum(expo, axis=1, keepdims=True)
        summed = summed + jnp.dot(
            expo.astype(jnp.bfloat16), value, preferred_element_type=jnp.float32
        )
    return summed / total, largest + jnp.log(total)


def column(index):
    return slice(index * HEAD, (index + 1) * HEAD)


def store_lane(ref, head, lane_value, first):
    lanes = lax.broadcasted_iota(jnp.int32, ref.shape, 1)
    before = jnp.where(first, jnp.full(ref.shape, NEG, jnp.float32), ref[...])
    for at, value in enumerate(lane_value):
        before = jnp.where(lanes == head + at, value, before)
    ref[...] = before


def parts_kernel(query_count, key_count, group, keep_ref, *refs):
    queries = refs[:query_count]
    keys = refs[query_count : query_count + key_count]
    values = refs[query_count + key_count : query_count + 2 * key_count]
    outs = refs[query_count + 2 * key_count :]
    step = pl.program_id(0)
    for at in range(query_count):
        keeps = [keep_ref[at * key_count + i] != 0 for i in range(key_count)]
        logs = []
        for head in range(group):
            cols = column(head)
            attended, log_total = softmax_part(
                queries[at][:, cols],
                [key[:, cols] for key in keys],
                [value[:, cols] for value in values],
                keeps,
            )
            outs[2 * at][:, cols] = attended.astype(outs[2 * at].dtype)
            logs.append(log_total)
        store_lane(outs[2 * at + 1], step * group, logs, step == 0)


def wide_spec(rows, group):
    return pl.BlockSpec((None, rows, group * HEAD), lambda step: (0, 0, step))


def lane_spec(rows):
    return pl.BlockSpec((rows, LANES), lambda step: (0, 0))


def parts(queries, keys, values, keeps, out_types):
    rows, width = queries[0].shape[1:]
    steps = width // HEAD // GROUP
    wide = wide_spec(rows, GROUP)
    blocks = len(queries) * len(keys)
    return pl.pallas_call(
        functools.partial(parts_kernel, len(queries), len(keys), GROUP),
        grid=(steps,),
        in_specs=[pl.BlockSpec(memory_space=pltpu.SMEM)]
        + [wide] * (len(queries) + 2 * len(keys)),
        out_specs=[wide, lane_spec(rows)] * len(queries),
        out_shape=[
            item
            for kind in out_types
            for item in (
                jax.ShapeDtypeStruct((1, rows, width), kind),
                jax.ShapeDtypeStruct((rows, LANES), jnp.float32),
            )
        ],
        cost_estimate=pl.CostEstimate(
            flops=4 * rows * rows * width * blocks,
            bytes_accessed=2 * rows * width * (2 * len(queries) + 2 * len(keys)),
            transcendentals=rows * rows * width // HEAD * blocks,
        ),
    )(keeps, *queries, *keys, *values)


def shares(logs):
    largest = functools.reduce(jnp.maximum, logs)
    expos = [jnp.exp(log - largest) for log in logs]
    total = sum(expos)
    return [expo / total for expo in expos], largest + jnp.log(total)


def merge_kernel(count, group, keep_ref, *refs):
    blocks, log_refs = refs[:count], refs[count : 2 * count]
    out_ref, out_log_ref = refs[2 * count :]
    step = pl.program_id(0)
    logs = [
        jnp.where(keep_ref[i] != 0, log_ref[...], NEG) for i, log_ref in enumerate(log_refs)
    ]
    weights, log_total = shares(logs)
    out_log_ref[...] = log_total
    shift = lax.rem(LANES - step * group, LANES)
    weights = [pltpu.roll(weight, shift, 1) for weight in weights]
    for head in range(group):
        cols = column(head)
        out_ref[:, cols] = sum(
            weight[:, head : head + 1] * block[:, cols].astype(jnp.float32)
            for weight, block in zip(weights, blocks)
        ).astype(out_ref.dtype)


def merged(blocks, logs, keeps, kind):
    rows, width = blocks[0].shape[1:]
    wide = wide_spec(rows, GROUP)
    lane = lane_spec(rows)
    return pl.pallas_call(
        functools.partial(merge_kernel, len(blocks), GROUP),
        grid=(width // HEAD // GROUP,),
        in_specs=[pl.BlockSpec(memory_space=pltpu.SMEM)]
        + [wide] * len(blocks)
        + [lane] * len(blocks),
        out_specs=[wide, lane],
        out_shape=[
            jax.ShapeDtypeStruct((1, rows, width), kind),
            jax.ShapeDtypeStruct((rows, LANES), jnp.float32),
        ],
        cost_estimate=pl.CostEstimate(
            flops=2 * rows * width * len(blocks),
            bytes_accessed=2 * rows * width * (len(blocks) + 1),
            transcendentals=0,
        ),
    )(keeps, *blocks, *logs)


def final_kernel(count, group, keep_ref, query_ref, key_ref, value_ref, *refs):
    blocks, log_refs, out_ref = refs[:count], refs[count : 2 * count], refs[2 * count]
    step = pl.program_id(0)
    shift = lax.rem(LANES - step * group, LANES)
    logs = [
        pltpu.roll(jnp.where(keep_ref[1 + i] != 0, log_ref[...], NEG), shift, 1)
        for i, log_ref in enumerate(log_refs)
    ]
    keep = keep_ref[0] != 0
    for head in range(group):
        cols = column(head)
        attended, log_own = softmax_part(
            query_ref[:, cols], [key_ref[:, cols]], [value_ref[:, cols]], [keep]
        )
        weights, _ = shares([log_own] + [log[:, head : head + 1] for log in logs])
        total = weights[0] * attended
        for weight, block in zip(weights[1:], blocks):
            total = total + weight * block[:, cols].astype(jnp.float32)
        out_ref[:, cols] = total.astype(out_ref.dtype)


def final(query, key, value, blocks, logs, keeps):
    rows, width = query.shape[1:]
    wide = wide_spec(rows, GROUP)
    lane = lane_spec(rows)
    return pl.pallas_call(
        functools.partial(final_kernel, len(blocks), GROUP),
        grid=(width // HEAD // GROUP,),
        in_specs=[pl.BlockSpec(memory_space=pltpu.SMEM)]
        + [wide] * (3 + len(blocks))
        + [lane] * len(blocks),
        out_specs=wide,
        out_shape=jax.ShapeDtypeStruct((1, rows, width), query.dtype),
        cost_estimate=pl.CostEstimate(
            flops=4 * rows * rows * width,
            bytes_accessed=2 * rows * width * (len(blocks) + 4),
            transcendentals=rows * rows * width // HEAD,
        ),
    )(keeps, query, key, value, *blocks, *logs)


def per_device(queries, keys, values, band):
    frames, bands = lax.axis_size("frame"), lax.axis_size("row")
    toward = [(f, (f + 2) % frames) if f % 2 else (f, (f - 2) % frames) for f in range(frames)]
    away = [(target, source) for source, target in toward]
    twin = [(f, f ^ 1) for f in range(frames)]
    even = [(r, r ^ 1) for r in range(bands)]
    odd = [(r, r + 1) for r in range(1, bands - 1, 2)]
    odd += [(target, source) for source, target in odd]

    key_one = lax.ppermute(keys, "frame", toward)
    value_one = lax.ppermute(values, "frame", toward)
    key_two = lax.ppermute(keys, "frame", away)
    value_two = lax.ppermute(values, "frame", away)
    query_twin = lax.ppermute(queries, "frame", twin)
    band_twin = lax.ppermute(band, "frame", twin)
    query_even = lax.ppermute(queries, "row", even)
    query_odd = lax.ppermute(queries, "row", odd)
    twin_even = lax.ppermute(query_twin, "row", even)
    twin_odd = lax.ppermute(query_twin, "row", odd)

    is_odd = lax.axis_index("frame") % 2 == 1
    row = lax.axis_index("row")
    own, other = band[0], band_twin[0]
    has_odd = ((row > 0) & (row < bands - 1)).astype(jnp.int32)
    one = jnp.int32(1)
    other_own = jnp.where(is_odd, other[3], other[1])
    other_one = jnp.where(is_odd, other[1], other[3])
    own_one = jnp.where(is_odd, own[0], own[4])
    own_two = jnp.where(is_odd, own[4], own[0])

    def flags(*items):
        return jnp.stack([jnp.asarray(item).astype(jnp.int32) for item in items])

    half = jnp.bfloat16
    beside = own[2] >= 1
    even_part, even_log, odd_part, odd_log = parts(
        [query_even, query_odd], [keys], [values], flags(beside, beside), [half, half]
    )
    from_even = lax.ppermute((even_part, even_log), "row", even)
    from_odd = lax.ppermute((odd_part, odd_log), "row", odd)

    keep_two = (other_own >= 1, other_one >= 1)
    tw_even, tw_even_log, tw_odd, tw_odd_log = parts(
        [twin_even, twin_odd],
        [keys, key_one],
        [values, value_one],
        flags(*keep_two, *keep_two),
        [half, half],
    )
    tw_from_even = lax.ppermute((tw_even, tw_even_log), "row", even)
    tw_from_odd = lax.ppermute((tw_odd, tw_odd_log), "row", odd)

    tw_part, tw_log, own_part, own_log = parts(
        [query_twin, queries],
        [keys, key_one],
        [values, value_one],
        flags(other_own >= 0, other_one >= 0, one, own_one >= 0),
        [jnp.float32, jnp.float32],
    )
    tw_all, tw_all_log = merged(
        [tw_part, tw_from_even[0], tw_from_odd[0]],
        [tw_log, tw_from_even[1], tw_from_odd[1]],
        flags(one, one, has_odd),
        half,
    )
    from_twin = lax.ppermute((tw_all, tw_all_log), "frame", twin)
    return final(
        queries,
        key_two,
        value_two,
        [own_part, from_even[0], from_odd[0], from_twin[0]],
        [own_log, from_even[1], from_odd[1], from_twin[1]],
        flags(own_two >= 0, one, one, has_odd, one),
    )


def solution(mesh):
    return jax.shard_map(
        per_device,
        mesh=mesh,
        in_specs=(
            P("frame", "row", None),
            P("frame", "row", None),
            P("frame", "row", None),
            P("frame", None),
        ),
        out_specs=P("frame", "row", None),
        check_vma=False,
    )
```

```python
import functools

import jax
import jax.numpy as jnp
from jax import lax
from jax.experimental import pallas as pl
from jax.experimental.pallas import tpu as pltpu
from jax.sharding import PartitionSpec as P


HEAD = 128
NEG = -1e30
RATE = HEAD ** (-0.5) * 1.4426950408889634
THIRD = 32
VMEM = pl.BlockSpec(memory_space=pltpu.VMEM)
SMEM = pl.BlockSpec(memory_space=pltpu.SMEM)
GRANT = pltpu.CompilerParams(vmem_limit_bytes=16 << 20)


def column(index):
    return slice(index * HEAD, (index + 1) * HEAD)


def raw_scores(key, query):
    return lax.dot_general(
        key, query, (((1,), (1,)), ((), ())), preferred_element_type=jnp.float32
    )


def weighted(value, weights):
    return lax.dot_general(
        value, weights, (((0,), (0,)), ((), ())), preferred_element_type=jnp.float32
    )


def softmax_rows(raw):
    largest = functools.reduce(
        jnp.maximum, [jnp.max(part, axis=0, keepdims=True) for part in raw]
    )
    expos = [jnp.exp2((part - largest) * RATE) for part in raw]
    total = sum(jnp.sum(expo, axis=0, keepdims=True) for expo in expos)
    return [expo.astype(jnp.bfloat16) for expo in expos], total, largest


def store_log(scratch, at, log, packed):
    if not packed:
        scratch[at : at + 1, :] = log
        return
    high = log.astype(jnp.bfloat16).astype(jnp.float32)
    middle = (log - high).astype(jnp.bfloat16).astype(jnp.float32)
    for place, part in enumerate((high, middle, log - high - middle)):
        scratch[place * THIRD + at : place * THIRD + at + 1, :] = part


def read_log(block, heads, packed):
    log = block[0, :, column(heads)].astype(jnp.float32)
    if not packed:
        return log
    return log + pltpu.roll(log, HEAD - THIRD, 1) + pltpu.roll(log, HEAD - 2 * THIRD, 1)


def parts_kernel(query_count, key_count, first, heads, kinds, keep_ref, *refs):
    queries = refs[:query_count]
    keys = refs[query_count : query_count + key_count]
    values = refs[query_count + key_count : query_count + 2 * key_count]
    outs = refs[query_count + 2 * key_count : -2]
    log_scratch, packed_scratch = refs[-2:]
    rows = queries[0].shape[1]
    wide = query_count * rows
    lane = lax.broadcasted_iota(jnp.int32, (1, wide), 1)
    biases = []
    for i in range(key_count):
        bias = jnp.zeros((1, wide), jnp.float32)
        for at in range(query_count):
            kept = jnp.where(keep_ref[at * key_count + i] != 0, 0.0, NEG)
            bias = jnp.where(lane >= at * rows, kept, bias)
        biases.append(bias)
    log_scratch[...] = jnp.zeros(log_scratch.shape, jnp.float32)
    packed_scratch[...] = jnp.zeros(packed_scratch.shape, jnp.float32)

    def score(n):
        cols = column(first + n)
        query = jnp.concatenate([ref[0, :, cols] for ref in queries], 0)
        return [raw_scores(key[0, :, cols], query) + bias for key, bias in zip(keys, biases)]

    def attend(n, weights, total, largest):
        cols = column(first + n)
        summed = sum(weighted(value[0, :, cols], part) for value, part in zip(values, weights))
        log = largest * RATE + jnp.log2(total)
        store_log(log_scratch, n, log, False)
        store_log(packed_scratch, n, log, True)
        normed = (summed * (1.0 / total)).T
        for at, out in enumerate(outs):
            out[0, :, column(n)] = normed[at * rows : (at + 1) * rows].astype(out.dtype)

    raw = score(0)
    before = None
    for n in range(heads):
        later = score(n + 1) if n + 1 < heads else None
        now = softmax_rows(raw)
        if before is not None:
            attend(n - 1, *before)
        before, raw = now, later
    attend(heads - 1, *before)
    logs = {False: log_scratch[...].T, True: packed_scratch[...].T}
    for at, (out, kind) in enumerate(zip(outs, kinds)):
        log = logs[kind == jnp.bfloat16][at * rows : (at + 1) * rows]
        out[0, :, column(heads)] = log.astype(out.dtype)


def parts(queries, keys, values, keeps, kinds, first, heads):
    rows = queries[0].shape[1]
    wide = len(queries) * rows
    blocks = len(queries) * len(keys)
    width = heads * HEAD
    return pl.pallas_call(
        functools.partial(parts_kernel, len(queries), len(keys), first, heads, kinds),
        in_specs=[SMEM] + [VMEM] * (len(queries) + 2 * len(keys)),
        out_specs=[VMEM] * len(queries),
        out_shape=[
            jax.ShapeDtypeStruct((1, rows, width + HEAD), kind) for kind in kinds
        ],
        scratch_shapes=[pltpu.VMEM((HEAD, wide), jnp.float32)] * 2,
        compiler_params=GRANT,
        cost_estimate=pl.CostEstimate(
            flops=4 * rows * rows * width * blocks,
            bytes_accessed=2 * rows * width * (2 * len(queries) + 2 * len(keys)),
            transcendentals=rows * rows * heads * blocks,
        ),
    )(keeps, *queries, *keys, *values)


def shares(logs):
    largest = functools.reduce(jnp.maximum, logs)
    expos = [jnp.exp2(log - largest) for log in logs]
    total = sum(expos)
    inverse = 1.0 / total
    return [expo * inverse for expo in expos], largest + jnp.log2(total)


def merge_kernel(heads, packs, keep_ref, *refs):
    blocks, out_ref = refs[:-1], refs[-1]
    logs = [
        jnp.where(keep_ref[i] != 0, read_log(block, heads, pack), NEG)
        for i, (block, pack) in enumerate(zip(blocks, packs))
    ]
    weights, log = shares(logs)
    for n in range(heads):
        cols = column(n)
        out_ref[0, :, cols] = sum(
            weight[:, n : n + 1] * block[0, :, cols].astype(jnp.float32)
            for weight, block in zip(weights, blocks)
        ).astype(out_ref.dtype)
    lane = lax.broadcasted_iota(jnp.int32, log.shape, 1)
    high = log.astype(jnp.bfloat16).astype(jnp.float32)
    middle = (log - high).astype(jnp.bfloat16).astype(jnp.float32)
    low = log - high - middle
    packed = jnp.where(
        lane < THIRD,
        high,
        jnp.where(
            lane < 2 * THIRD, pltpu.roll(middle, THIRD, 1), pltpu.roll(low, 2 * THIRD, 1)
        ),
    )
    out_ref[0, :, column(heads)] = packed.astype(out_ref.dtype)


def merged(blocks, keeps):
    rows, width = blocks[0].shape[1:]
    heads = width // HEAD - 1
    packs = tuple(block.dtype == jnp.bfloat16 for block in blocks)
    return pl.pallas_call(
        functools.partial(merge_kernel, heads, packs),
        in_specs=[SMEM] + [VMEM] * len(blocks),
        out_specs=VMEM,
        out_shape=jax.ShapeDtypeStruct((1, rows, width), jnp.bfloat16),
        compiler_params=GRANT,
        cost_estimate=pl.CostEstimate(
            flops=2 * rows * width * len(blocks),
            bytes_accessed=2 * rows * width * (len(blocks) + 1),
            transcendentals=0,
        ),
    )(keeps, *blocks)


def absorb_kernel(heads, groups, last, keep_ref, query_ref, key_ref, value_ref, *refs):
    count = sum(len(group) for group in groups)
    pieces, out_ref = refs[:count], refs[count]
    weight_scratch, log_scratch, share_scratch, coef_scratch = refs[count + 1 :]
    rows = query_ref.shape[1]
    bias = jnp.where(keep_ref[0] != 0, 0.0, NEG)
    place = []
    at = 0
    for i, group in enumerate(groups):
        total_log = jnp.zeros((rows, HEAD), jnp.float32)
        lane = lax.broadcasted_iota(jnp.int32, (rows, HEAD), 1)
        where = {}
        for start, size, pack in group:
            log = read_log(pieces[at], size, pack)
            if start:
                log = pltpu.roll(log, start, 1)
            total_log = jnp.where(lane >= start, log, total_log)
            for n in range(size):
                where[start + n] = (at, n)
            at += 1
        log_scratch[i] = jnp.where(keep_ref[1 + i] != 0, total_log, NEG).T
        place.append(where)

    def score(n):
        return [raw_scores(key_ref[0, :, column(n)], query_ref[0, :, column(n)]) + bias]

    raw = score(0)
    for n in range(heads):
        later = score(n + 1) if n + 1 < heads else None
        (weights,), total, largest = softmax_rows(raw)
        weight_scratch[n] = weights
        logs = [log_scratch[i, n : n + 1, :] for i in range(len(groups))]
        portions, log = shares([largest * RATE + jnp.log2(total)] + logs)
        coef_scratch[n : n + 1, :] = portions[0] * (1.0 / total)
        for i, portion in enumerate(portions[1:]):
            share_scratch[i, n : n + 1, :] = portion
        if not last:
            log_scratch[0, n : n + 1, :] = log
        raw = later
    columns = [share_scratch[i].T for i in range(len(groups))]
    for n in range(heads):
        cols = column(n)
        summed = weighted(value_ref[0, :, cols], weight_scratch[n])
        out = (summed * coef_scratch[n : n + 1, :]).T
        for i in range(len(groups)):
            piece, index = place[i][n]
            block = pieces[piece][0, :, column(index)].astype(jnp.float32)
            out = out + columns[i][:, n : n + 1] * block
        out_ref[0, :, cols] = out.astype(out_ref.dtype)
    if not last:
        out_ref[0, :, column(heads)] = log_scratch[0].T


def absorbed(query, key, value, groups, keeps, last):
    rows, width = query.shape[1:]
    heads = width // HEAD
    kind = query.dtype if last else jnp.float32
    shapes, pieces = [], []
    for group in groups:
        shape, start = [], 0
        for piece in group:
            size = piece.shape[2] // HEAD - 1
            shape.append((start, size, piece.dtype == jnp.bfloat16))
            start += size
            pieces.append(piece)
        shapes.append(tuple(shape))
    table = pltpu.VMEM((len(groups), HEAD, rows), jnp.float32)
    return pl.pallas_call(
        functools.partial(absorb_kernel, heads, tuple(shapes), last),
        in_specs=[SMEM] + [VMEM] * (3 + len(pieces)),
        out_specs=VMEM,
        out_shape=jax.ShapeDtypeStruct((1, rows, width + (0 if last else HEAD)), kind),
        scratch_shapes=[
            pltpu.VMEM((heads, rows, rows), jnp.bfloat16),
            table,
            table,
            pltpu.VMEM((HEAD, rows), jnp.float32),
        ],
        compiler_params=GRANT,
        cost_estimate=pl.CostEstimate(
            flops=4 * rows * rows * width,
            bytes_accessed=2 * rows * width * (len(pieces) + 4),
            transcendentals=rows * rows * heads,
        ),
    )(keeps, query, key, value, *pieces)


def per_device(queries, keys, values, band):
    frames, bands = lax.axis_size("frame"), lax.axis_size("row")
    toward = [(f, (f + 2) % frames) if f % 2 else (f, (f - 2) % frames) for f in range(frames)]
    away = [(target, source) for source, target in toward]
    twin = [(f, f ^ 1) for f in range(frames)]
    even = [(r, r ^ 1) for r in range(bands)]
    odd = [(r, r + 1) for r in range(1, bands - 1, 2)]
    odd += [(target, source) for source, target in odd]

    key_one = lax.ppermute(keys, "frame", toward)
    value_one = lax.ppermute(values, "frame", toward)
    key_two = lax.ppermute(keys, "frame", away)
    value_two = lax.ppermute(values, "frame", away)
    query_twin = lax.ppermute(queries, "frame", twin)
    band_twin = lax.ppermute(band, "frame", twin)
    query_even = lax.ppermute(queries, "row", even)
    query_odd = lax.ppermute(queries, "row", odd)
    twin_even = lax.ppermute(query_twin, "row", even)
    twin_odd = lax.ppermute(query_twin, "row", odd)

    is_odd = lax.axis_index("frame") % 2 == 1
    row = lax.axis_index("row")
    own, other = band[0], band_twin[0]
    has_odd = (row > 0) & (row < bands - 1)
    other_own = jnp.where(is_odd, other[3], other[1])
    other_one = jnp.where(is_odd, other[1], other[3])
    own_one = jnp.where(is_odd, own[0], own[4])
    own_two = jnp.where(is_odd, own[4], own[0])

    def flags(*items):
        return jnp.stack([jnp.asarray(item).astype(jnp.int32) for item in items])

    narrow, full = jnp.bfloat16, jnp.float32
    heads = queries.shape[2] // HEAD
    spans = [(0, heads // 2), (heads // 2, heads - heads // 2)]

    beside = own[2] >= 1
    even_part, odd_part, own_part = parts(
        [query_even, query_odd, queries],
        [keys],
        [values],
        flags(beside, beside, True),
        (narrow, narrow, full),
        0,
        heads,
    )
    from_even = lax.ppermute(even_part, "row", even)
    from_odd = lax.ppermute(odd_part, "row", odd)

    keep_beside = (other_own >= 1, other_one >= 1)
    keep_other = flags(*keep_beside, *keep_beside, other_own >= 0, other_one >= 0)
    from_twin = []
    for first, size in spans:
        even_twin, odd_twin, own_twin = parts(
            [twin_even, twin_odd, query_twin],
            [keys, key_one],
            [values, value_one],
            keep_other,
            (narrow, narrow, full),
            first,
            size,
        )
        back_even = lax.ppermute(even_twin, "row", even)
        back_odd = lax.ppermute(odd_twin, "row", odd)
        whole = merged([own_twin, back_even, back_odd], flags(True, True, has_odd))
        from_twin.append(lax.ppermute(whole, "frame", twin))

    near = absorbed(
        queries,
        key_one,
        value_one,
        [[own_part], [from_even], [from_odd]],
        flags(own_one >= 0, True, True, has_odd),
        False,
    )
    return absorbed(
        queries,
        key_two,
        value_two,
        [[near], from_twin],
        flags(own_two >= 0, True, True),
        True,
    )


def solution(mesh):
    return jax.shard_map(
        per_device,
        mesh=mesh,
        in_specs=(
            P("frame", "row", None),
            P("frame", "row", None),
            P("frame", "row", None),
            P("frame", None),
        ),
        out_specs=P("frame", "row", None),
        check_vma=False,
    )
```

```python
import functools

import jax
import jax.numpy as jnp
from jax import lax
from jax.experimental import pallas as pl
from jax.experimental.pallas import tpu as pltpu
from jax.sharding import PartitionSpec as P


HEAD = 128
NEG = -1e30
RATE = HEAD ** (-0.5) * 1.4426950408889634
THIRD = 32
VMEM = pl.BlockSpec(memory_space=pltpu.VMEM)
SMEM = pl.BlockSpec(memory_space=pltpu.SMEM)
GRANT = pltpu.CompilerParams(vmem_limit_bytes=16 << 20)


def column(index):
    return slice(index * HEAD, (index + 1) * HEAD)


def raw_scores(key, query):
    return lax.dot_general(
        key, query, (((1,), (1,)), ((), ())), preferred_element_type=jnp.float32
    )


def weighted(value, weights):
    return lax.dot_general(
        value, weights, (((0,), (0,)), ((), ())), preferred_element_type=jnp.float32
    )


def softmax_rows(raw):
    largest = functools.reduce(
        jnp.maximum, [jnp.max(part, axis=0, keepdims=True) for part in raw]
    )
    expos = [jnp.exp2((part - largest) * RATE) for part in raw]
    total = sum(jnp.sum(expo, axis=0, keepdims=True) for expo in expos)
    return [expo.astype(jnp.bfloat16) for expo in expos], total, largest


def thirds(value):
    high = value.astype(jnp.bfloat16).astype(jnp.float32)
    middle = (value - high).astype(jnp.bfloat16).astype(jnp.float32)
    return high, middle, value - high - middle


def packed(value):
    lane = lax.broadcasted_iota(jnp.int32, value.shape, 1)
    high, middle, low = thirds(value)
    rest = jnp.where(
        lane < 2 * THIRD, pltpu.roll(middle, THIRD, 1), pltpu.roll(low, 2 * THIRD, 1)
    )
    return jnp.where(lane < THIRD, high, rest).astype(jnp.bfloat16)


def read_log(block, heads):
    log = block[0, :, column(heads)].astype(jnp.float32)
    if block.dtype == jnp.float32:
        return log
    return log + pltpu.roll(log, HEAD - THIRD, 1) + pltpu.roll(log, HEAD - 2 * THIRD, 1)


def spread(table, n):
    row = lax.broadcasted_iota(jnp.int32, (HEAD, HEAD), 0)
    chosen = (row == n) | (row == THIRD + n) | (row == 2 * THIRD + n)
    return jnp.dot(
        table,
        jnp.where(chosen, 1.0, 0.0).astype(jnp.bfloat16),
        preferred_element_type=jnp.float32,
    )


def shares(logs):
    largest = functools.reduce(jnp.maximum, logs)
    expos = [jnp.exp2(log - largest) for log in logs]
    total = sum(expos)
    inverse = 1.0 / total
    return [expo * inverse for expo in expos], largest + jnp.log2(total)


def kept(rule, band_ref, twin_ref):
    odd_frame = lax.axis_index("frame") % 2 == 1
    row = lax.axis_index("row")
    return rule(
        [band_ref[0, i] for i in range(5)],
        [twin_ref[0, i] for i in range(5)] if twin_ref is not None else None,
        odd_frame,
        (row > 0) & (row < lax.axis_size("row") - 1),
    )


def parts_kernel(query_count, key_count, first, heads, rule, *refs):
    band_ref, twin_ref, refs = refs[0], refs[1], refs[2:]
    queries = refs[:query_count]
    keys = refs[query_count : query_count + key_count]
    values = refs[query_count + key_count : query_count + 2 * key_count]
    outs = refs[query_count + 2 * key_count : -1]
    log_scratch = refs[-1]
    rows = queries[0].shape[1]
    wide = query_count * rows
    lane = lax.broadcasted_iota(jnp.int32, (1, wide), 1)
    keeps = kept(rule, band_ref, twin_ref)
    biases = []
    for i in range(key_count):
        bias = jnp.zeros((1, wide), jnp.float32)
        for at in range(query_count):
            if keeps[at][i] is not True:
                bias = jnp.where(
                    (lane >= at * rows) & (lane < (at + 1) * rows),
                    jnp.where(keeps[at][i], 0.0, NEG),
                    bias,
                )
        biases.append(bias)
    log_scratch[...] = jnp.zeros(log_scratch.shape, jnp.float32)

    def of(ref, n):
        start = 0 if ref.shape[2] == heads * HEAD else first
        return ref[0, :, column(start + n)]

    def score(n):
        query = jnp.concatenate([of(ref, n) for ref in queries], 0)
        return [raw_scores(of(key, n), query) + bias for key, bias in zip(keys, biases)]

    def attend(n, weights, total, largest):
        summed = sum(weighted(of(value, n), part) for value, part in zip(values, weights))
        log_scratch[n : n + 1, :] = largest * RATE + jnp.log2(total)
        normed = (summed * (1.0 / total)).T
        for at, out in enumerate(outs):
            out[0, :, column(n)] = normed[at * rows : (at + 1) * rows].astype(out.dtype)

    raw = score(0)
    before = None
    for n in range(heads):
        later = score(n + 1) if n + 1 < heads else None
        now = softmax_rows(raw)
        if before is not None:
            attend(n - 1, *before)
        before, raw = now, later
    attend(heads - 1, *before)
    logs = log_scratch[...].T
    for at, out in enumerate(outs):
        log = logs[at * rows : (at + 1) * rows]
        out[0, :, column(heads)] = log if out.dtype == jnp.float32 else packed(log)


def parts(bands, queries, keys, values, rule, kinds, first, heads):
    rows = queries[0].shape[1]
    wide = len(queries) * rows
    blocks = len(queries) * len(keys)
    width = heads * HEAD
    return pl.pallas_call(
        functools.partial(parts_kernel, len(queries), len(keys), first, heads, rule),
        in_specs=[SMEM] * 2 + [VMEM] * (len(queries) + 2 * len(keys)),
        out_specs=[VMEM] * len(queries),
        out_shape=[
            jax.ShapeDtypeStruct((1, rows, width + HEAD), kind) for kind in kinds
        ],
        scratch_shapes=[pltpu.VMEM((HEAD, wide), jnp.float32)],
        compiler_params=GRANT,
        cost_estimate=pl.CostEstimate(
            flops=4 * rows * rows * width * blocks,
            bytes_accessed=2 * rows * width * (2 * len(queries) + 2 * len(keys)),
            transcendentals=rows * rows * heads * blocks,
        ),
    )(*bands, *queries, *keys, *values)


def merge_kernel(heads, rule, band_ref, *refs):
    blocks, out_ref = refs[:-1], refs[-1]
    keeps = kept(rule, band_ref, None)
    logs = []
    for keep, block in zip(keeps, blocks):
        log = read_log(block, heads)
        logs.append(log if keep is True else jnp.where(keep, log, NEG))
    weights, log = shares(logs)
    tables = [packed(weight) for weight in weights]
    for n in range(heads):
        cols = column(n)
        out_ref[0, :, cols] = sum(
            spread(table, n) * block[0, :, cols].astype(jnp.float32)
            for table, block in zip(tables, blocks)
        ).astype(out_ref.dtype)
    out_ref[0, :, column(heads)] = packed(log)


def merged(band, blocks, rule):
    rows, width = blocks[0].shape[1:]
    heads = width // HEAD - 1
    return pl.pallas_call(
        functools.partial(merge_kernel, heads, rule),
        in_specs=[SMEM] + [VMEM] * len(blocks),
        out_specs=VMEM,
        out_shape=jax.ShapeDtypeStruct((1, rows, width), jnp.bfloat16),
        compiler_params=GRANT,
        cost_estimate=pl.CostEstimate(
            flops=2 * rows * width * len(blocks),
            bytes_accessed=2 * rows * width * (len(blocks) + 1),
            transcendentals=0,
        ),
    )(band, *blocks)


def score_kernel(rule, band_ref, query_ref, *refs):
    keys, (weight_ref, table_ref, scratch) = refs[:-3], refs[-3:]
    bias = jnp.where(kept(rule, band_ref, None)[0], 0.0, NEG)
    places = [(key, n) for key in keys for n in range(key.shape[2] // HEAD)]
    scratch[...] = jnp.zeros(scratch.shape, jnp.float32)

    def score(at):
        key, n = places[at]
        return [raw_scores(key[0, :, column(n)], query_ref[0, :, column(at)]) + bias]

    raw = score(0)
    for n in range(len(places)):
        later = score(n + 1) if n + 1 < len(places) else None
        (weights,), total, largest = softmax_rows(raw)
        weight_ref[n] = weights
        scratch[0, n : n + 1, :] = largest * RATE + jnp.log2(total)
        scratch[1, n : n + 1, :] = 1.0 / total
        raw = later
    table_ref[0] = scratch[0].T
    table_ref[1] = scratch[1].T


def scored(band, query, keys, rule):
    rows, width = query.shape[1:]
    heads = width // HEAD
    return pl.pallas_call(
        functools.partial(score_kernel, rule),
        in_specs=[SMEM] + [VMEM] * (1 + len(keys)),
        out_specs=[VMEM] * 2,
        out_shape=[
            jax.ShapeDtypeStruct((heads, rows, rows), jnp.bfloat16),
            jax.ShapeDtypeStruct((2, rows, HEAD), jnp.float32),
        ],
        scratch_shapes=[pltpu.VMEM((2, HEAD, rows), jnp.float32)],
        compiler_params=GRANT,
        cost_estimate=pl.CostEstimate(
            flops=2 * rows * rows * width,
            bytes_accessed=6 * rows * width,
            transcendentals=rows * rows * heads,
        ),
    )(band, query, *keys)


def combine_kernel(value_count, groups, heads, rule, last, band_ref, weight_ref, table_ref, *refs):
    values, refs = refs[:value_count], refs[value_count:]
    pieces, out_ref = refs[:-1], refs[-1]
    keeps = kept(rule, band_ref, None)
    rows = out_ref.shape[1]
    lane = lax.broadcasted_iota(jnp.int32, (rows, HEAD), 1)
    value_at = [(value, n) for value in values for n in range(value.shape[2] // HEAD)]
    logs = [table_ref[0]]
    places = []
    at = 0
    for keep, group in zip(keeps, groups):
        log = None
        place = []
        for size in group:
            part = read_log(pieces[at], size)
            if log is None:
                log = part
            else:
                log = jnp.where(lane >= len(place), pltpu.roll(part, len(place), 1), log)
            place += [(at, n) for n in range(size)]
            at += 1
        logs.append(log if keep is True else jnp.where(keep, log, NEG))
        places.append(place)
    weights, log = shares(logs)
    weights[0] = weights[0] * table_ref[1]
    tables = [packed(weight) for weight in weights]
    for n in range(heads):
        value, index = value_at[n]
        out = weighted(value[0, :, column(index)], weight_ref[n]).T * spread(tables[0], n)
        for table, place in zip(tables[1:], places):
            piece, index = place[n]
            block = pieces[piece][0, :, column(index)].astype(jnp.float32)
            out = out + spread(table, n) * block
        out_ref[0, :, column(n)] = out.astype(out_ref.dtype)
    if not last:
        out_ref[0, :, column(heads)] = log


def combined(band, score, values, groups, rule, last):
    weights, table = score
    heads, rows = weights.shape[:2]
    width = heads * HEAD
    kind = values[0].dtype if last else jnp.float32
    sizes = tuple(tuple(piece.shape[2] // HEAD - 1 for piece in group) for group in groups)
    pieces = [piece for group in groups for piece in group]
    return pl.pallas_call(
        functools.partial(combine_kernel, len(values), sizes, heads, rule, last),
        in_specs=[SMEM] + [VMEM] * (2 + len(values) + len(pieces)),
        out_specs=VMEM,
        out_shape=jax.ShapeDtypeStruct((1, rows, width + (0 if last else HEAD)), kind),
        compiler_params=GRANT,
        cost_estimate=pl.CostEstimate(
            flops=2 * rows * rows * width,
            bytes_accessed=2 * rows * width * (len(pieces) + 4),
            transcendentals=0,
        ),
    )(band, weights, table, *values, *pieces)


def per_device(queries, keys, values, band):
    frames, bands = lax.axis_size("frame"), lax.axis_size("row")
    toward = [(f, (f + 2) % frames) if f % 2 else (f, (f - 2) % frames) for f in range(frames)]
    away = [(target, source) for source, target in toward]
    twin = [(f, f ^ 1) for f in range(frames)]
    even = [(r, r ^ 1) for r in range(bands)]
    odd = [(r, r + 1) for r in range(1, bands - 1, 2)]
    odd += [(target, source) for source, target in odd]

    narrow, full = jnp.bfloat16, jnp.float32
    heads = queries.shape[2] // HEAD
    half = heads // 2
    spans = [(0, half), (half, heads - half)]

    near = []
    for first, size in spans:
        cut = slice(first * HEAD, (first + size) * HEAD)
        near.append(
            (
                lax.ppermute(keys[:, :, cut], "frame", toward),
                lax.ppermute(values[:, :, cut], "frame", toward),
            )
        )
    key_two = lax.ppermute(keys, "frame", away)
    value_two = lax.ppermute(values, "frame", away)
    query_twin = []
    for first, size in spans:
        cut = slice(first * HEAD, (first + size) * HEAD)
        query_twin.append(lax.ppermute(queries[:, :, cut], "frame", twin))
    band_twin = lax.ppermute(band, "frame", twin)
    query_even = lax.ppermute(queries, "row", even)
    query_odd = lax.ppermute(queries, "row", odd)
    twin_even = [lax.ppermute(query_twin[span], "row", even) for span in (0, 1)]
    twin_odd = [lax.ppermute(query_twin[span], "row", odd) for span in (0, 1)]

    def beside_rule(own, other, odd_frame, has_odd):
        return [[own[2] >= 1], [own[2] >= 1], [True]]

    even_part, odd_part, own_part = parts(
        (band, band),
        [query_even, query_odd, queries],
        [keys],
        [values],
        beside_rule,
        (narrow, narrow, full),
        0,
        heads,
    )
    from_even = lax.ppermute(even_part, "row", even)
    from_odd = lax.ppermute(odd_part, "row", odd)

    def twin_rule(own, other, odd_frame, has_odd):
        here = jnp.where(odd_frame, other[3], other[1])
        there = jnp.where(odd_frame, other[1], other[3])
        beside = [here >= 1, there >= 1]
        return [beside, beside, [here >= 0, there >= 0]]

    from_twin = []
    for span, (first, size) in enumerate(spans):
        even_twin, odd_twin, own_twin = parts(
            (band, band_twin),
            [twin_even[span], twin_odd[span], query_twin[span]],
            [keys, near[span][0]],
            [values, near[span][1]],
            twin_rule,
            (narrow, narrow, full),
            first,
            size,
        )
        back_even = lax.ppermute(even_twin, "row", even)
        back_odd = lax.ppermute(odd_twin, "row", odd)
        whole = merged(
            band,
            [own_twin, back_even, back_odd],
            lambda own, other, odd_frame, has_odd: [True, True, has_odd],
        )
        from_twin.append(lax.ppermute(whole, "frame", twin))

    near_score = scored(
        band,
        queries,
        [pair[0] for pair in near],
        lambda own, other, odd_frame, has_odd: [jnp.where(odd_frame, own[0], own[4]) >= 0],
    )
    near_all = combined(
        band,
        near_score,
        [pair[1] for pair in near],
        [[own_part], [from_even], [from_odd]],
        lambda own, other, odd_frame, has_odd: [True, True, has_odd],
        False,
    )
    far_score = scored(
        band,
        queries,
        [key_two],
        lambda own, other, odd_frame, has_odd: [jnp.where(odd_frame, own[4], own[0]) >= 0],
    )
    return combined(
        band,
        far_score,
        [value_two],
        [[near_all], from_twin],
        lambda own, other, odd_frame, has_odd: [True, True],
        True,
    )


def solution(mesh):
    return jax.shard_map(
        per_device,
        mesh=mesh,
        in_specs=(
            P("frame", "row", None),
            P("frame", "row", None),
            P("frame", "row", None),
            P("frame", None),
        ),
        out_specs=P("frame", "row", None),
        check_vma=False,
    )
```

```python
import functools

import jax
import jax.numpy as jnp
from jax import lax
from jax.experimental import pallas as pl
from jax.experimental.pallas import tpu as pltpu
from jax.sharding import PartitionSpec as P


HEAD = 128
NEG = -1e30
RATE = HEAD ** (-0.5) * 1.4426950408889634
THIRD = 32
BATCH = 5
VMEM = pl.BlockSpec(memory_space=pltpu.VMEM)
SMEM = pl.BlockSpec(memory_space=pltpu.SMEM)
HBM = pl.BlockSpec(memory_space=pltpu.HBM)
GRANT = pltpu.CompilerParams(vmem_limit_bytes=16 << 20)


def column(index):
    return slice(index * HEAD, (index + 1) * HEAD)


def raw_scores(key, query):
    return lax.dot_general(
        key, query, (((1,), (1,)), ((), ())), preferred_element_type=jnp.float32
    )


def weighted(value, weights):
    return lax.dot_general(
        value, weights, (((0,), (0,)), ((), ())), preferred_element_type=jnp.float32
    )


def softmax_rows(raw):
    largest = functools.reduce(
        jnp.maximum, [jnp.max(part, axis=0, keepdims=True) for part in raw]
    )
    expos = [jnp.exp2((part - largest) * RATE) for part in raw]
    total = sum(jnp.sum(expo, axis=0, keepdims=True) for expo in expos)
    return [expo.astype(jnp.bfloat16) for expo in expos], total, largest


def thirds(value):
    high = value.astype(jnp.bfloat16).astype(jnp.float32)
    middle = (value - high).astype(jnp.bfloat16).astype(jnp.float32)
    return high, middle, value - high - middle


def packed(value):
    lane = lax.broadcasted_iota(jnp.int32, value.shape, 1)
    high, middle, low = thirds(value)
    rest = jnp.where(
        lane < 2 * THIRD, pltpu.roll(middle, THIRD, 1), pltpu.roll(low, 2 * THIRD, 1)
    )
    return jnp.where(lane < THIRD, high, rest).astype(jnp.bfloat16)


def read_log(block, heads):
    log = block[0, :, column(heads)].astype(jnp.float32)
    if block.dtype == jnp.float32:
        return log
    return log + pltpu.roll(log, HEAD - THIRD, 1) + pltpu.roll(log, HEAD - 2 * THIRD, 1)


def spread(table, n):
    row = lax.broadcasted_iota(jnp.int32, (HEAD, HEAD), 0)
    chosen = (row == n) | (row == THIRD + n) | (row == 2 * THIRD + n)
    return jnp.dot(
        table,
        jnp.where(chosen, 1.0, 0.0).astype(jnp.bfloat16),
        preferred_element_type=jnp.float32,
    )


def shares(logs):
    largest = functools.reduce(jnp.maximum, logs)
    expos = [jnp.exp2(log - largest) for log in logs]
    total = sum(expos)
    inverse = 1.0 / total
    return [expo * inverse for expo in expos], largest + jnp.log2(total)


def kept(rule, band_ref, twin_ref):
    odd_frame = lax.axis_index("frame") % 2 == 1
    row = lax.axis_index("row")
    return rule(
        [band_ref[0, i] for i in range(5)],
        [twin_ref[0, i] for i in range(5)] if twin_ref is not None else None,
        odd_frame,
        (row > 0) & (row < lax.axis_size("row") - 1),
    )


def parts_kernel(query_count, key_count, first, heads, rule, *refs):
    band_ref, twin_ref, refs = refs[0], refs[1], refs[2:]
    queries = refs[:query_count]
    keys = refs[query_count : query_count + key_count]
    values = refs[query_count + key_count : query_count + 2 * key_count]
    outs = refs[query_count + 2 * key_count : -1]
    log_scratch = refs[-1]
    rows = queries[0].shape[1]
    wide = query_count * rows
    lane = lax.broadcasted_iota(jnp.int32, (1, wide), 1)
    keeps = kept(rule, band_ref, twin_ref)
    biases = []
    for i in range(key_count):
        bias = jnp.zeros((1, wide), jnp.float32)
        for at in range(query_count):
            if keeps[at][i] is not True:
                bias = jnp.where(
                    (lane >= at * rows) & (lane < (at + 1) * rows),
                    jnp.where(keeps[at][i], 0.0, NEG),
                    bias,
                )
        biases.append(bias)
    log_scratch[...] = jnp.zeros(log_scratch.shape, jnp.float32)

    def of(ref, n):
        start = 0 if ref.shape[2] == heads * HEAD else first
        return ref[0, :, column(start + n)]

    def score(n):
        query = jnp.concatenate([of(ref, n) for ref in queries], 0)
        return [raw_scores(of(key, n), query) + bias for key, bias in zip(keys, biases)]

    def attend(n, weights, total, largest):
        summed = sum(weighted(of(value, n), part) for value, part in zip(values, weights))
        log_scratch[n : n + 1, :] = largest * RATE + jnp.log2(total)
        normed = (summed * (1.0 / total)).T
        for at, out in enumerate(outs):
            out[0, :, column(n)] = normed[at * rows : (at + 1) * rows].astype(out.dtype)

    raw = score(0)
    before = None
    for n in range(heads):
        later = score(n + 1) if n + 1 < heads else None
        now = softmax_rows(raw)
        if before is not None:
            attend(n - 1, *before)
        before, raw = now, later
    attend(heads - 1, *before)
    logs = log_scratch[...].T
    for at, out in enumerate(outs):
        log = logs[at * rows : (at + 1) * rows]
        out[0, :, column(heads)] = log if out.dtype == jnp.float32 else packed(log)


def parts(bands, queries, keys, values, rule, kinds, first, heads):
    rows = queries[0].shape[1]
    wide = len(queries) * rows
    blocks = len(queries) * len(keys)
    width = heads * HEAD
    return pl.pallas_call(
        functools.partial(parts_kernel, len(queries), len(keys), first, heads, rule),
        in_specs=[SMEM] * 2 + [VMEM] * (len(queries) + 2 * len(keys)),
        out_specs=[VMEM] * len(queries),
        out_shape=[
            jax.ShapeDtypeStruct((1, rows, width + HEAD), kind) for kind in kinds
        ],
        scratch_shapes=[pltpu.VMEM((HEAD, wide), jnp.float32)],
        compiler_params=GRANT,
        cost_estimate=pl.CostEstimate(
            flops=4 * rows * rows * width * blocks,
            bytes_accessed=2 * rows * width * (2 * len(queries) + 2 * len(keys)),
            transcendentals=rows * rows * heads * blocks,
        ),
    )(*bands, *queries, *keys, *values)


def merge_kernel(heads, rule, band_ref, *refs):
    blocks, out_ref = refs[:-1], refs[-1]
    keeps = kept(rule, band_ref, None)
    logs = []
    for keep, block in zip(keeps, blocks):
        log = read_log(block, heads)
        logs.append(log if keep is True else jnp.where(keep, log, NEG))
    weights, log = shares(logs)
    tables = [packed(weight) for weight in weights]
    for n in range(heads):
        cols = column(n)
        out_ref[0, :, cols] = sum(
            spread(table, n) * block[0, :, cols].astype(jnp.float32)
            for table, block in zip(tables, blocks)
        ).astype(out_ref.dtype)
    out_ref[0, :, column(heads)] = packed(log)


def merged(band, blocks, rule):
    rows, width = blocks[0].shape[1:]
    heads = width // HEAD - 1
    return pl.pallas_call(
        functools.partial(merge_kernel, heads, rule),
        in_specs=[SMEM] + [VMEM] * len(blocks),
        out_specs=VMEM,
        out_shape=jax.ShapeDtypeStruct((1, rows, width), jnp.bfloat16),
        compiler_params=GRANT,
        cost_estimate=pl.CostEstimate(
            flops=2 * rows * width * len(blocks),
            bytes_accessed=2 * rows * width * (len(blocks) + 1),
            transcendentals=0,
        ),
    )(band, *blocks)


def score_kernel(rule, band_ref, query_ref, *refs):
    keys, (weight_ref, table_ref, scratch) = refs[:-3], refs[-3:]
    bias = jnp.where(kept(rule, band_ref, None)[0], 0.0, NEG)
    places = [(key, n) for key in keys for n in range(key.shape[2] // HEAD)]
    scratch[...] = jnp.zeros(scratch.shape, jnp.float32)

    def score(at):
        key, n = places[at]
        return [raw_scores(key[0, :, column(n)], query_ref[0, :, column(at)]) + bias]

    raw = score(0)
    for n in range(len(places)):
        later = score(n + 1) if n + 1 < len(places) else None
        (weights,), total, largest = softmax_rows(raw)
        weight_ref[n] = weights
        scratch[0, n : n + 1, :] = largest * RATE + jnp.log2(total)
        scratch[1, n : n + 1, :] = 1.0 / total
        raw = later
    table_ref[0] = scratch[0].T
    table_ref[1] = scratch[1].T


def scored(band, query, keys, rule):
    rows, width = query.shape[1:]
    heads = width // HEAD
    return pl.pallas_call(
        functools.partial(score_kernel, rule),
        in_specs=[SMEM] + [VMEM] * (1 + len(keys)),
        out_specs=[VMEM] * 2,
        out_shape=[
            jax.ShapeDtypeStruct((heads, rows, rows), jnp.bfloat16),
            jax.ShapeDtypeStruct((2, rows, HEAD), jnp.float32),
        ],
        scratch_shapes=[pltpu.VMEM((2, HEAD, rows), jnp.float32)],
        compiler_params=GRANT,
        cost_estimate=pl.CostEstimate(
            flops=2 * rows * rows * width,
            bytes_accessed=6 * rows * width,
            transcendentals=rows * rows * heads,
        ),
    )(band, query, *keys)


def blend_kernel(value_count, groups, heads, rule, band_ref, weight_ref, table_ref, *refs):
    values, refs = refs[:value_count], refs[value_count:]
    pieces, out_ref = refs[: sum(len(group) for group in groups)], refs[-2]
    keeps = kept(rule, band_ref, None)
    rows = out_ref.shape[1]
    lane = lax.broadcasted_iota(jnp.int32, (rows, HEAD), 1)
    value_at = [(value, n) for value in values for n in range(value.shape[2] // HEAD)]
    logs = [table_ref[0]]
    places = []
    at = 0
    for keep, group in zip(keeps, groups):
        log = None
        place = []
        for size in group:
            part = read_log(pieces[at], size)
            if log is None:
                log = part
            else:
                log = jnp.where(lane >= len(place), pltpu.roll(part, len(place), 1), log)
            place += [(at, n) for n in range(size)]
            at += 1
        logs.append(log if keep is True else jnp.where(keep, log, NEG))
        places.append(place)
    weights, log = shares(logs)
    coef = (weights[0] * table_ref[1]).T
    refs[-1][...] = coef
    if values:
        out_ref[0, :, column(heads)] = log
    tables = [packed(weight) for weight in weights[1:]]
    for n in range(heads):
        out = 0.0
        if values:
            value, index = value_at[n]
            summed = weighted(value[0, :, column(index)], weight_ref[n])
            out = (summed * refs[-1][n : n + 1, :]).T
        for table, place in zip(tables, places):
            piece, index = place[n]
            block = pieces[piece][0, :, column(index)].astype(jnp.float32)
            out = out + spread(table, n) * block
        out_ref[0, :, column(n)] = out


def blended(band, score, values, groups, rule):
    weights, table = score
    heads, rows = weights.shape[:2]
    width = heads * HEAD
    sizes = tuple(tuple(piece.shape[2] // HEAD - 1 for piece in group) for group in groups)
    pieces = [piece for group in groups for piece in group]
    out_shape = jax.ShapeDtypeStruct((1, rows, width + (HEAD if values else 0)), jnp.float32)
    coef = jax.ShapeDtypeStruct((HEAD, rows), jnp.float32)
    if not values:
        weights = table
    out = pl.pallas_call(
        functools.partial(blend_kernel, len(values), sizes, heads, rule),
        in_specs=[SMEM] + [VMEM] * (2 + len(values) + len(pieces)),
        out_specs=[VMEM] if values else [VMEM, VMEM],
        out_shape=[out_shape] if values else [out_shape, coef],
        scratch_shapes=[pltpu.VMEM(coef.shape, coef.dtype)] if values else [],
        compiler_params=GRANT,
        cost_estimate=pl.CostEstimate(
            flops=2 * rows * rows * width,
            bytes_accessed=2 * rows * width * (len(pieces) + 4),
            transcendentals=0,
        ),
    )(band, weights, table, *values, *pieces)
    return out[0] if values else out


def final_kernel(first, heads, weight_ref, coef_ref, value_ref, base_ref, *refs):
    out_ref, scratch, sems = refs[-3:]
    copies = []
    for n in range(heads):
        cols = column(first + n)
        summed = weighted(value_ref[0, :, column(n)], weight_ref[first + n])
        out = (summed * coef_ref[first + n : first + n + 1, :]).T + base_ref[0, :, cols]
        scratch[:, column(n)] = out.astype(scratch.dtype)
        if (n + 1) % BATCH == 0 or n + 1 == heads:
            start = n // BATCH * BATCH
            done = slice(start * HEAD, (n + 1) * HEAD)
            target = slice((first + start) * HEAD, (first + n + 1) * HEAD)
            copy = pltpu.make_async_copy(
                scratch.at[:, done], out_ref.at[0, :, target], sems.at[n // BATCH]
            )
            copy.start()
            copies.append(copy)
    for copy in copies:
        copy.wait()


def finished(weights, coef, value, base, whole, first):
    rows, width = base.shape[1:]
    heads = value.shape[2] // HEAD
    return pl.pallas_call(
        functools.partial(final_kernel, first, heads),
        in_specs=[VMEM] * 4 + [HBM] * (whole is not None),
        out_specs=HBM,
        out_shape=jax.ShapeDtypeStruct((1, rows, width), value.dtype),
        scratch_shapes=[
            pltpu.VMEM((rows, heads * HEAD), value.dtype),
            pltpu.SemaphoreType.DMA((-(-heads // BATCH),)),
        ],
        input_output_aliases={4: 0} if whole is not None else {},
        compiler_params=GRANT,
        cost_estimate=pl.CostEstimate(
            flops=2 * rows * rows * heads * HEAD,
            bytes_accessed=8 * rows * heads * HEAD,
            transcendentals=0,
        ),
    )(weights, coef, value, base, *([] if whole is None else [whole]))


def per_device(queries, keys, values, band):
    frames, bands = lax.axis_size("frame"), lax.axis_size("row")
    toward = [(f, (f + 2) % frames) if f % 2 else (f, (f - 2) % frames) for f in range(frames)]
    away = [(target, source) for source, target in toward]
    twin = [(f, f ^ 1) for f in range(frames)]
    even = [(r, r ^ 1) for r in range(bands)]
    odd = [(r, r + 1) for r in range(1, bands - 1, 2)]
    odd += [(target, source) for source, target in odd]

    narrow, full = jnp.bfloat16, jnp.float32
    heads = queries.shape[2] // HEAD
    half = heads // 2
    spans = [(0, half), (half, heads - half)]

    cuts = [slice(first * HEAD, (first + size) * HEAD) for first, size in spans]
    value_halves = [values[:, :, cut] for cut in cuts]

    key_one = lax.ppermute(keys, "frame", toward)
    value_one = [lax.ppermute(value_halves[span], "frame", toward) for span in (0, 1)]
    key_two = lax.ppermute(keys, "frame", away)
    value_two = [lax.ppermute(value_halves[span], "frame", away) for span in (0, 1)]
    query_twin = []
    for cut in cuts:
        query_twin.append(lax.ppermute(queries[:, :, cut], "frame", twin))
    band_twin = lax.ppermute(band, "frame", twin)
    query_even = lax.ppermute(queries, "row", even)
    query_odd = lax.ppermute(queries, "row", odd)
    twin_even = [lax.ppermute(query_twin[span], "row", even) for span in (0, 1)]
    twin_odd = [lax.ppermute(query_twin[span], "row", odd) for span in (0, 1)]

    def beside_rule(own, other, odd_frame, has_odd):
        return [[own[2] >= 1], [own[2] >= 1], [True]]

    even_part, odd_part, own_part = parts(
        (band, band),
        [query_even, query_odd, queries],
        [keys],
        [values],
        beside_rule,
        (narrow, narrow, full),
        0,
        heads,
    )
    from_even = lax.ppermute(even_part, "row", even)
    from_odd = lax.ppermute(odd_part, "row", odd)

    def twin_rule(own, other, odd_frame, has_odd):
        here = jnp.where(odd_frame, other[3], other[1])
        there = jnp.where(odd_frame, other[1], other[3])
        beside = [here >= 1, there >= 1]
        return [beside, beside, [here >= 0, there >= 0]]

    from_twin = []
    for span, (first, size) in enumerate(spans):
        even_twin, odd_twin, own_twin = parts(
            (band, band_twin),
            [twin_even[span], twin_odd[span], query_twin[span]],
            [keys, key_one],
            [values, value_one[span]],
            twin_rule,
            (narrow, narrow, full),
            first,
            size,
        )
        back_even = lax.ppermute(even_twin, "row", even)
        back_odd = lax.ppermute(odd_twin, "row", odd)
        whole = merged(
            band,
            [own_twin, back_even, back_odd],
            lambda own, other, odd_frame, has_odd: [True, True, has_odd],
        )
        from_twin.append(lax.ppermute(whole, "frame", twin))

    near_score = scored(
        band,
        queries,
        [key_one],
        lambda own, other, odd_frame, has_odd: [jnp.where(odd_frame, own[0], own[4]) >= 0],
    )
    near = blended(
        band,
        near_score,
        value_one,
        [[own_part], [from_even], [from_odd]],
        lambda own, other, odd_frame, has_odd: [True, True, has_odd],
    )
    far_score = scored(
        band,
        queries,
        [key_two],
        lambda own, other, odd_frame, has_odd: [jnp.where(odd_frame, own[4], own[0]) >= 0],
    )
    base, coef = blended(
        band,
        far_score,
        [],
        [[near], from_twin],
        lambda own, other, odd_frame, has_odd: [True, True],
    )
    out = None
    for span, (first, size) in enumerate(spans):
        out = finished(far_score[0], coef, value_two[span], base, out, first)
    return out


def solution(mesh):
    return jax.shard_map(
        per_device,
        mesh=mesh,
        in_specs=(
            P("frame", "row", None),
            P("frame", "row", None),
            P("frame", "row", None),
            P("frame", None),
        ),
        out_specs=P("frame", "row", None),
        check_vma=False,
    )
```

```python
import functools

import jax
import jax.numpy as jnp
from jax import lax
from jax.experimental import pallas as pl
from jax.experimental.pallas import tpu as pltpu
from jax.sharding import PartitionSpec as P


HEAD = 128
NEG = -1e30
RATE = HEAD ** (-0.5) * 1.4426950408889634
THIRD = 32
BATCH = 5
VMEM = pl.BlockSpec(memory_space=pltpu.VMEM)
SMEM = pl.BlockSpec(memory_space=pltpu.SMEM)
HBM = pl.BlockSpec(memory_space=pltpu.HBM)
GRANT = pltpu.CompilerParams(vmem_limit_bytes=16 << 20)


def column(index):
    return slice(index * HEAD, (index + 1) * HEAD)


def raw_scores(key, query):
    return lax.dot_general(
        key, query, (((1,), (1,)), ((), ())), preferred_element_type=jnp.float32
    )


def weighted(value, weights):
    return lax.dot_general(
        value, weights, (((0,), (0,)), ((), ())), preferred_element_type=jnp.float32
    )


def softmax_rows(raw):
    largest = functools.reduce(
        jnp.maximum, [jnp.max(part, axis=0, keepdims=True) for part in raw]
    )
    expos = [jnp.exp2((part - largest) * RATE) for part in raw]
    total = sum(jnp.sum(expo, axis=0, keepdims=True) for expo in expos)
    return [expo.astype(jnp.bfloat16) for expo in expos], total, largest


def thirds(value):
    high = value.astype(jnp.bfloat16).astype(jnp.float32)
    middle = (value - high).astype(jnp.bfloat16).astype(jnp.float32)
    return high, middle, value - high - middle


def packed(value):
    lane = lax.broadcasted_iota(jnp.int32, value.shape, 1)
    high, middle, low = thirds(value)
    rest = jnp.where(
        lane < 2 * THIRD, pltpu.roll(middle, THIRD, 1), pltpu.roll(low, 2 * THIRD, 1)
    )
    return jnp.where(lane < THIRD, high, rest).astype(jnp.bfloat16)


def read_log(block, heads):
    log = block[0, :, column(heads)].astype(jnp.float32)
    if block.dtype == jnp.float32:
        return log
    return log + pltpu.roll(log, HEAD - THIRD, 1) + pltpu.roll(log, HEAD - 2 * THIRD, 1)


def spread(table, n):
    row = lax.broadcasted_iota(jnp.int32, (HEAD, HEAD), 0)
    chosen = (row == n) | (row == THIRD + n) | (row == 2 * THIRD + n)
    return jnp.dot(
        table,
        jnp.where(chosen, 1.0, 0.0).astype(jnp.bfloat16),
        preferred_element_type=jnp.float32,
    )


def shares(logs):
    largest = functools.reduce(jnp.maximum, logs)
    expos = [jnp.exp2(log - largest) for log in logs]
    total = sum(expos)
    inverse = 1.0 / total
    return [expo * inverse for expo in expos], largest + jnp.log2(total)


def kept(rule, band_ref, twin_ref):
    odd_frame = lax.axis_index("frame") % 2 == 1
    row = lax.axis_index("row")
    return rule(
        [band_ref[0, i] for i in range(5)],
        [twin_ref[0, i] for i in range(5)] if twin_ref is not None else None,
        odd_frame,
        (row > 0) & (row < lax.axis_size("row") - 1),
    )


def grouped(refs, sizes):
    groups, at = [], 0
    for size in sizes:
        groups.append(refs[at : at + size])
        at += size
    return groups


def parts_kernel(query_count, key_count, shares_of, first, heads, rule, *refs):
    band_ref, twin_ref, refs = refs[0], refs[1], refs[2:]
    queries = refs[:query_count]
    keys = refs[query_count : query_count + key_count]
    values = grouped(refs[query_count + key_count : query_count + key_count + sum(shares_of)], shares_of)
    outs = refs[query_count + key_count + sum(shares_of) : -1]
    log_scratch = refs[-1]
    rows = queries[0].shape[1]
    wide = query_count * rows
    lane = lax.broadcasted_iota(jnp.int32, (1, wide), 1)
    keeps = kept(rule, band_ref, twin_ref)
    biases = []
    for i in range(key_count):
        bias = jnp.zeros((1, wide), jnp.float32)
        for at in range(query_count):
            if keeps[at][i] is not True:
                bias = jnp.where(
                    (lane >= at * rows) & (lane < (at + 1) * rows),
                    jnp.where(keeps[at][i], 0.0, NEG),
                    bias,
                )
        biases.append(bias)
    log_scratch[...] = jnp.zeros(log_scratch.shape, jnp.float32)

    def of(ref, n):
        start = 0 if ref.shape[2] == heads * HEAD else first
        return ref[0, :, column(start + n)]

    def score(n):
        query = jnp.concatenate([of(ref, n) for ref in queries], 0)
        return [raw_scores(of(key, n), query) + bias for key, bias in zip(keys, biases)]

    def attend(n, weights, total, largest):
        summed = sum(
            weighted(sum(of(ref, n) for ref in value), part)
            for value, part in zip(values, weights)
        )
        log_scratch[n : n + 1, :] = largest * RATE + jnp.log2(total)
        normed = (summed * (1.0 / total)).T
        for at, out in enumerate(outs):
            out[0, :, column(n)] = normed[at * rows : (at + 1) * rows].astype(out.dtype)

    raw = score(0)
    before = None
    for n in range(heads):
        later = score(n + 1) if n + 1 < heads else None
        now = softmax_rows(raw)
        if before is not None:
            attend(n - 1, *before)
        before, raw = now, later
    attend(heads - 1, *before)
    logs = log_scratch[...].T
    for at, out in enumerate(outs):
        log = logs[at * rows : (at + 1) * rows]
        out[0, :, column(heads)] = log if out.dtype == jnp.float32 else packed(log)


def parts(bands, queries, keys, values, rule, kinds, first, heads):
    rows = queries[0].shape[1]
    wide = len(queries) * rows
    blocks = len(queries) * len(keys)
    width = heads * HEAD
    shares_of = tuple(len(value) for value in values)
    flat = [piece for value in values for piece in value]
    return pl.pallas_call(
        functools.partial(
            parts_kernel, len(queries), len(keys), shares_of, first, heads, rule
        ),
        in_specs=[SMEM] * 2 + [VMEM] * (len(queries) + len(keys) + len(flat)),
        out_specs=[VMEM] * len(queries),
        out_shape=[
            jax.ShapeDtypeStruct((1, rows, width + HEAD), kind) for kind in kinds
        ],
        scratch_shapes=[pltpu.VMEM((HEAD, wide), jnp.float32)],
        compiler_params=GRANT,
        cost_estimate=pl.CostEstimate(
            flops=4 * rows * rows * width * blocks,
            bytes_accessed=2 * rows * width * (2 * len(queries) + 2 * len(keys)),
            transcendentals=rows * rows * heads * blocks,
        ),
    )(*bands, *queries, *keys, *flat)


def merge_kernel(heads, rule, band_ref, *refs):
    blocks, out_ref = refs[:-1], refs[-1]
    keeps = kept(rule, band_ref, None)
    logs = []
    for keep, block in zip(keeps, blocks):
        log = read_log(block, heads)
        logs.append(log if keep is True else jnp.where(keep, log, NEG))
    weights, log = shares(logs)
    tables = [packed(weight) for weight in weights]
    for n in range(heads):
        cols = column(n)
        out_ref[0, :, cols] = sum(
            spread(table, n) * block[0, :, cols].astype(jnp.float32)
            for table, block in zip(tables, blocks)
        ).astype(out_ref.dtype)
    out_ref[0, :, column(heads)] = packed(log)


def merged(band, blocks, rule):
    rows, width = blocks[0].shape[1:]
    heads = width // HEAD - 1
    return pl.pallas_call(
        functools.partial(merge_kernel, heads, rule),
        in_specs=[SMEM] + [VMEM] * len(blocks),
        out_specs=VMEM,
        out_shape=jax.ShapeDtypeStruct((1, rows, width), jnp.bfloat16),
        compiler_params=GRANT,
        cost_estimate=pl.CostEstimate(
            flops=2 * rows * width * len(blocks),
            bytes_accessed=2 * rows * width * (len(blocks) + 1),
            transcendentals=0,
        ),
    )(band, *blocks)


def score_kernel(rule, upright, band_ref, query_ref, *refs):
    keys, (weight_ref, table_ref, scratch) = refs[:-3], refs[-3:]
    bias = jnp.where(kept(rule, band_ref, None)[0], 0.0, NEG)
    places = [(key, n) for key in keys for n in range(key.shape[2] // HEAD)]
    scratch[...] = jnp.zeros(scratch.shape, jnp.float32)

    def score(at):
        key, n = places[at]
        return [raw_scores(key[0, :, column(n)], query_ref[0, :, column(at)]) + bias]

    raw = score(0)
    for n in range(len(places)):
        later = score(n + 1) if n + 1 < len(places) else None
        (weights,), total, largest = softmax_rows(raw)
        weight_ref[n] = weights.T if upright else weights
        scratch[0, n : n + 1, :] = largest * RATE + jnp.log2(total)
        scratch[1, n : n + 1, :] = 1.0 / total
        raw = later
    table_ref[0] = scratch[0].T
    table_ref[1] = scratch[1].T


def scored(band, query, keys, rule, upright):
    rows, width = query.shape[1:]
    heads = width // HEAD
    return pl.pallas_call(
        functools.partial(score_kernel, rule, upright),
        in_specs=[SMEM] + [VMEM] * (1 + len(keys)),
        out_specs=[VMEM] * 2,
        out_shape=[
            jax.ShapeDtypeStruct((heads, rows, rows), jnp.bfloat16),
            jax.ShapeDtypeStruct((2, rows, HEAD), jnp.float32),
        ],
        scratch_shapes=[pltpu.VMEM((2, HEAD, rows), jnp.float32)],
        compiler_params=GRANT,
        cost_estimate=pl.CostEstimate(
            flops=2 * rows * rows * width,
            bytes_accessed=6 * rows * width,
            transcendentals=rows * rows * heads,
        ),
    )(band, query, *keys)


def blend_kernel(shares_of, groups, heads, rule, band_ref, weight_ref, table_ref, *refs):
    values, refs = grouped(refs[: sum(shares_of)], shares_of), refs[sum(shares_of) :]
    pieces, out_ref = refs[: sum(len(group) for group in groups)], refs[-2]
    keeps = kept(rule, band_ref, None)
    rows = out_ref.shape[1]
    lane = lax.broadcasted_iota(jnp.int32, (rows, HEAD), 1)
    value_at = [(value, n) for value in values for n in range(value[0].shape[2] // HEAD)]
    logs = [table_ref[0]]
    places = []
    at = 0
    for keep, group in zip(keeps, groups):
        log = None
        place = []
        for size in group:
            part = read_log(pieces[at], size)
            if log is None:
                log = part
            else:
                log = jnp.where(lane >= len(place), pltpu.roll(part, len(place), 1), log)
            place += [(at, n) for n in range(size)]
            at += 1
        logs.append(log if keep is True else jnp.where(keep, log, NEG))
        places.append(place)
    weights, log = shares(logs)
    coef = weights[0] * table_ref[1]
    if values:
        refs[-1][...] = coef.T
        out_ref[0, :, column(heads)] = log
    else:
        refs[-1][...] = packed(coef)
    tables = [packed(weight) for weight in weights[1:]]
    for n in range(heads):
        out = 0.0
        if values:
            value, index = value_at[n]
            summed = weighted(sum(ref[0, :, column(index)] for ref in value), weight_ref[n])
            out = (summed * refs[-1][n : n + 1, :]).T
        for table, place in zip(tables, places):
            piece, index = place[n]
            block = pieces[piece][0, :, column(index)].astype(jnp.float32)
            out = out + spread(table, n) * block
        out_ref[0, :, column(n)] = out


def blended(band, score, values, groups, rule):
    weights, table = score
    heads, rows = weights.shape[:2]
    width = heads * HEAD
    sizes = tuple(tuple(piece.shape[2] // HEAD - 1 for piece in group) for group in groups)
    pieces = [piece for group in groups for piece in group]
    out_shape = jax.ShapeDtypeStruct((1, rows, width + (HEAD if values else 0)), jnp.float32)
    coef = jax.ShapeDtypeStruct((rows, HEAD), jnp.bfloat16)
    shares_of = tuple(len(value) for value in values)
    flat = [piece for value in values for piece in value]
    if not values:
        weights = table
    out = pl.pallas_call(
        functools.partial(blend_kernel, shares_of, sizes, heads, rule),
        in_specs=[SMEM] + [VMEM] * (2 + len(flat) + len(pieces)),
        out_specs=[VMEM] if values else [VMEM, VMEM],
        out_shape=[out_shape] if values else [out_shape, coef],
        scratch_shapes=[pltpu.VMEM((HEAD, rows), jnp.float32)] if values else [],
        compiler_params=GRANT,
        cost_estimate=pl.CostEstimate(
            flops=2 * rows * rows * width,
            bytes_accessed=2 * rows * width * (len(pieces) + 4),
            transcendentals=0,
        ),
    )(band, weights, table, *flat, *pieces)
    return out[0] if values else out


def final_kernel(first, heads, weight_ref, coef_ref, value_ref, base_ref, *refs):
    out_ref, scratch, sems = refs[-3:]
    copies = []
    for n in range(heads):
        cols = column(first + n)
        summed = jnp.dot(
            weight_ref[first + n],
            value_ref[0, :, column(n)],
            preferred_element_type=jnp.float32,
        )
        out = summed * spread(coef_ref[...], first + n) + base_ref[0, :, cols]
        scratch[:, column(n)] = out.astype(scratch.dtype)
        if (n + 1) % BATCH == 0 or n + 1 == heads:
            start = n // BATCH * BATCH
            done = slice(start * HEAD, (n + 1) * HEAD)
            target = slice((first + start) * HEAD, (first + n + 1) * HEAD)
            copy = pltpu.make_async_copy(
                scratch.at[:, done], out_ref.at[0, :, target], sems.at[n // BATCH]
            )
            copy.start()
            copies.append(copy)
    for copy in copies:
        copy.wait()


def finished(weights, coef, value, base, whole, first):
    rows, width = base.shape[1:]
    heads = value.shape[2] // HEAD
    return pl.pallas_call(
        functools.partial(final_kernel, first, heads),
        in_specs=[VMEM] * 4 + [HBM] * (whole is not None),
        out_specs=HBM,
        out_shape=jax.ShapeDtypeStruct((1, rows, width), value.dtype),
        scratch_shapes=[
            pltpu.VMEM((rows, heads * HEAD), value.dtype),
            pltpu.SemaphoreType.DMA((-(-heads // BATCH),)),
        ],
        input_output_aliases={4: 0} if whole is not None else {},
        compiler_params=GRANT,
        cost_estimate=pl.CostEstimate(
            flops=2 * rows * rows * heads * HEAD,
            bytes_accessed=8 * rows * heads * HEAD,
            transcendentals=0,
        ),
    )(weights, coef, value, base, *([] if whole is None else [whole]))


def per_device(queries, keys, values, band):
    frames, bands = lax.axis_size("frame"), lax.axis_size("row")
    toward = [(f, (f + 2) % frames) if f % 2 else (f, (f - 2) % frames) for f in range(frames)]
    away = [(target, source) for source, target in toward]
    twin = [(f, f ^ 1) for f in range(frames)]
    even = [(r, r ^ 1) for r in range(bands)]
    odd = [(r, r + 1) for r in range(1, bands - 1, 2)]
    odd += [(target, source) for source, target in odd]

    narrow, full = jnp.bfloat16, jnp.float32
    heads = queries.shape[2] // HEAD
    half = heads // 2
    spans = [(0, half), (half, heads - half)]

    cuts = [slice(first * HEAD, (first + size) * HEAD) for first, size in spans]
    value_halves = [values[:, :, cut] for cut in cuts]
    tail = (heads - half) // 5 * 2
    ends = [0, half, heads - tail, heads]
    value_thirds = value_halves[:1] + [
        values[:, :, start * HEAD : stop * HEAD] for start, stop in zip(ends[1:], ends[2:])
    ]
    beyond = [(a, b) for a, b in toward if abs(a - b) != 2]
    within = [(a, b) for a, b in toward if abs(a - b) == 2]

    key_one = lax.ppermute(keys, "frame", toward)
    value_one = [
        (lax.ppermute(value_halves[0], "frame", toward),),
        (
            lax.ppermute(value_halves[1], "frame", within),
            lax.ppermute(value_halves[1], "frame", beyond),
        ),
    ]
    key_two = lax.ppermute(keys, "frame", away)
    value_two = [lax.ppermute(piece, "frame", away) for piece in value_thirds]
    query_twin = []
    for cut in cuts:
        query_twin.append(lax.ppermute(queries[:, :, cut], "frame", twin))
    band_twin = lax.ppermute(band, "frame", twin)
    query_even = lax.ppermute(queries, "row", even)
    query_odd = lax.ppermute(queries, "row", odd)
    twin_even = [lax.ppermute(query_twin[span], "row", even) for span in (0, 1)]
    twin_odd = [lax.ppermute(query_twin[span], "row", odd) for span in (0, 1)]

    def beside_rule(own, other, odd_frame, has_odd):
        return [[own[2] >= 1], [own[2] >= 1], [True]]

    even_part, odd_part, own_part = parts(
        (band, band),
        [query_even, query_odd, queries],
        [keys],
        [(values,)],
        beside_rule,
        (narrow, narrow, full),
        0,
        heads,
    )
    from_even = lax.ppermute(even_part, "row", even)
    from_odd = lax.ppermute(odd_part, "row", odd)

    def twin_rule(own, other, odd_frame, has_odd):
        here = jnp.where(odd_frame, other[3], other[1])
        there = jnp.where(odd_frame, other[1], other[3])
        beside = [here >= 1, there >= 1]
        return [beside, beside, [here >= 0, there >= 0]]

    from_twin = []
    for span, (first, size) in enumerate(spans):
        even_twin, odd_twin, own_twin = parts(
            (band, band_twin),
            [twin_even[span], twin_odd[span], query_twin[span]],
            [keys, key_one],
            [(values,), value_one[span]],
            twin_rule,
            (narrow, narrow, full),
            first,
            size,
        )
        back_even = lax.ppermute(even_twin, "row", even)
        back_odd = lax.ppermute(odd_twin, "row", odd)
        whole = merged(
            band,
            [own_twin, back_even, back_odd],
            lambda own, other, odd_frame, has_odd: [True, True, has_odd],
        )
        from_twin.append(lax.ppermute(whole, "frame", twin))

    near_score = scored(
        band,
        queries,
        [key_one],
        lambda own, other, odd_frame, has_odd: [jnp.where(odd_frame, own[0], own[4]) >= 0],
        False,
    )
    near = blended(
        band,
        near_score,
        value_one,
        [[own_part], [from_even], [from_odd]],
        lambda own, other, odd_frame, has_odd: [True, True, has_odd],
    )
    far_score = scored(
        band,
        queries,
        [key_two],
        lambda own, other, odd_frame, has_odd: [jnp.where(odd_frame, own[4], own[0]) >= 0],
        True,
    )
    base, coef = blended(
        band,
        far_score,
        [],
        [[near], from_twin],
        lambda own, other, odd_frame, has_odd: [True, True],
    )
    out = None
    for at, first in enumerate(ends[:-1]):
        out = finished(far_score[0], coef, value_two[at], base, out, first)
    return out


def solution(mesh):
    return jax.shard_map(
        per_device,
        mesh=mesh,
        in_specs=(
            P("frame", "row", None),
            P("frame", "row", None),
            P("frame", "row", None),
            P("frame", None),
        ),
        out_specs=P("frame", "row", None),
        check_vma=False,
    )
```

```python
import functools

import jax
import jax.numpy as jnp
from jax import lax
from jax.experimental import pallas as pl
from jax.experimental.pallas import tpu as pltpu
from jax.sharding import PartitionSpec as P


HEAD = 128
NEG = -1e30
RATE = HEAD ** (-0.5) * 1.4426950408889634
THIRD = 32
BATCH = 5
VMEM = pl.BlockSpec(memory_space=pltpu.VMEM)
SMEM = pl.BlockSpec(memory_space=pltpu.SMEM)
HBM = pl.BlockSpec(memory_space=pltpu.HBM)
GRANT = pltpu.CompilerParams(vmem_limit_bytes=16 << 20)


def column(index):
    return slice(index * HEAD, (index + 1) * HEAD)


def raw_scores(key, query):
    return lax.dot_general(
        key, query, (((1,), (1,)), ((), ())), preferred_element_type=jnp.float32
    )


def weighted(value, weights):
    return lax.dot_general(
        value, weights, (((0,), (0,)), ((), ())), preferred_element_type=jnp.float32
    )


def softmax_rows(raw):
    largest = functools.reduce(
        jnp.maximum, [jnp.max(part, axis=0, keepdims=True) for part in raw]
    )
    expos = [jnp.exp2((part - largest) * RATE) for part in raw]
    total = sum(jnp.sum(expo, axis=0, keepdims=True) for expo in expos)
    return [expo.astype(jnp.bfloat16) for expo in expos], total, largest


def thirds(value):
    high = value.astype(jnp.bfloat16).astype(jnp.float32)
    middle = (value - high).astype(jnp.bfloat16).astype(jnp.float32)
    return high, middle, value - high - middle


def packed(value):
    lane = lax.broadcasted_iota(jnp.int32, value.shape, 1)
    high, middle, low = thirds(value)
    rest = jnp.where(
        lane < 2 * THIRD, pltpu.roll(middle, THIRD, 1), pltpu.roll(low, 2 * THIRD, 1)
    )
    return jnp.where(lane < THIRD, high, rest).astype(jnp.bfloat16)


def read_log(block, heads):
    log = block[0, :, column(heads)].astype(jnp.float32)
    if block.dtype == jnp.float32:
        return log
    return log + pltpu.roll(log, HEAD - THIRD, 1) + pltpu.roll(log, HEAD - 2 * THIRD, 1)


def spread(table, n):
    row = lax.broadcasted_iota(jnp.int32, (HEAD, HEAD), 0)
    chosen = (row == n) | (row == THIRD + n) | (row == 2 * THIRD + n)
    return jnp.dot(
        table,
        jnp.where(chosen, 1.0, 0.0).astype(jnp.bfloat16),
        preferred_element_type=jnp.float32,
    )


def shares(logs):
    largest = functools.reduce(jnp.maximum, logs)
    expos = [jnp.exp2(log - largest) for log in logs]
    total = sum(expos)
    inverse = 1.0 / total
    return [expo * inverse for expo in expos], largest + jnp.log2(total)


def kept(rule, band_ref, twin_ref):
    odd_frame = lax.axis_index("frame") % 2 == 1
    row = lax.axis_index("row")
    return rule(
        [band_ref[0, i] for i in range(5)],
        [twin_ref[0, i] for i in range(5)] if twin_ref is not None else None,
        odd_frame,
        (row > 0) & (row < lax.axis_size("row") - 1),
    )


def grouped(refs, sizes):
    groups, at = [], 0
    for size in sizes:
        groups.append(refs[at : at + size])
        at += size
    return groups


def parts_kernel(query_count, key_count, shares_of, first, heads, rule, *refs):
    band_ref, twin_ref, refs = refs[0], refs[1], refs[2:]
    queries = refs[:query_count]
    keys = refs[query_count : query_count + key_count]
    values = grouped(refs[query_count + key_count : query_count + key_count + sum(shares_of)], shares_of)
    outs = refs[query_count + key_count + sum(shares_of) : -1]
    log_scratch = refs[-1]
    rows = queries[0].shape[1]
    wide = query_count * rows
    lane = lax.broadcasted_iota(jnp.int32, (1, wide), 1)
    keeps = kept(rule, band_ref, twin_ref)
    biases = []
    for i in range(key_count):
        bias = jnp.zeros((1, wide), jnp.float32)
        for at in range(query_count):
            if keeps[at][i] is not True:
                bias = jnp.where(
                    (lane >= at * rows) & (lane < (at + 1) * rows),
                    jnp.where(keeps[at][i], 0.0, NEG),
                    bias,
                )
        biases.append(bias)
    log_scratch[...] = jnp.zeros(log_scratch.shape, jnp.float32)

    def of(ref, n):
        start = 0 if ref.shape[2] == heads * HEAD else first
        return ref[0, :, column(start + n)]

    def score(n):
        query = jnp.concatenate([of(ref, n) for ref in queries], 0)
        return [raw_scores(of(key, n), query) + bias for key, bias in zip(keys, biases)]

    def attend(n, weights, total, largest):
        summed = sum(
            weighted(sum(of(ref, n) for ref in value), part)
            for value, part in zip(values, weights)
        )
        log_scratch[n : n + 1, :] = largest * RATE + jnp.log2(total)
        normed = (summed * (1.0 / total)).T
        for at, out in enumerate(outs):
            out[0, :, column(n)] = normed[at * rows : (at + 1) * rows].astype(out.dtype)

    raw = score(0)
    before = None
    for n in range(heads):
        later = score(n + 1) if n + 1 < heads else None
        now = softmax_rows(raw)
        if before is not None:
            attend(n - 1, *before)
        before, raw = now, later
    attend(heads - 1, *before)
    logs = log_scratch[...].T
    for at, out in enumerate(outs):
        log = logs[at * rows : (at + 1) * rows]
        out[0, :, column(heads)] = log if out.dtype == jnp.float32 else packed(log)


def parts(bands, queries, keys, values, rule, kinds, first, heads):
    rows = queries[0].shape[1]
    wide = len(queries) * rows
    blocks = len(queries) * len(keys)
    width = heads * HEAD
    shares_of = tuple(len(value) for value in values)
    flat = [piece for value in values for piece in value]
    return pl.pallas_call(
        functools.partial(
            parts_kernel, len(queries), len(keys), shares_of, first, heads, rule
        ),
        in_specs=[SMEM] * 2 + [VMEM] * (len(queries) + len(keys) + len(flat)),
        out_specs=[VMEM] * len(queries),
        out_shape=[
            jax.ShapeDtypeStruct((1, rows, width + HEAD), kind) for kind in kinds
        ],
        scratch_shapes=[pltpu.VMEM((HEAD, wide), jnp.float32)],
        compiler_params=GRANT,
        cost_estimate=pl.CostEstimate(
            flops=4 * rows * rows * width * blocks,
            bytes_accessed=2 * rows * width * (2 * len(queries) + 2 * len(keys)),
            transcendentals=rows * rows * heads * blocks,
        ),
    )(*bands, *queries, *keys, *flat)


def merge_kernel(heads, rule, band_ref, *refs):
    blocks, out_ref = refs[:-1], refs[-1]
    keeps = kept(rule, band_ref, None)
    logs = []
    for keep, block in zip(keeps, blocks):
        log = read_log(block, heads)
        logs.append(log if keep is True else jnp.where(keep, log, NEG))
    weights, log = shares(logs)
    tables = [packed(weight) for weight in weights]
    for n in range(heads):
        cols = column(n)
        out_ref[0, :, cols] = sum(
            spread(table, n) * block[0, :, cols].astype(jnp.float32)
            for table, block in zip(tables, blocks)
        ).astype(out_ref.dtype)
    out_ref[0, :, column(heads)] = packed(log)


def merged(band, blocks, rule):
    rows, width = blocks[0].shape[1:]
    heads = width // HEAD - 1
    return pl.pallas_call(
        functools.partial(merge_kernel, heads, rule),
        in_specs=[SMEM] + [VMEM] * len(blocks),
        out_specs=VMEM,
        out_shape=jax.ShapeDtypeStruct((1, rows, width), jnp.bfloat16),
        compiler_params=GRANT,
        cost_estimate=pl.CostEstimate(
            flops=2 * rows * width * len(blocks),
            bytes_accessed=2 * rows * width * (len(blocks) + 1),
            transcendentals=0,
        ),
    )(band, *blocks)


def score_kernel(rule, band_ref, query_ref, *refs):
    keys, (weight_ref, table_ref, scratch) = refs[:-3], refs[-3:]
    bias = jnp.where(kept(rule, band_ref, None)[0], 0.0, NEG)
    places = [(key, n) for key in keys for n in range(key.shape[2] // HEAD)]
    scratch[...] = jnp.zeros(scratch.shape, jnp.float32)

    def score(at):
        key, n = places[at]
        return [raw_scores(key[0, :, column(n)], query_ref[0, :, column(at)]) + bias]

    raw = score(0)
    for n in range(len(places)):
        later = score(n + 1) if n + 1 < len(places) else None
        (weights,), total, largest = softmax_rows(raw)
        weight_ref[n] = weights.T
        scratch[0, n : n + 1, :] = largest * RATE + jnp.log2(total)
        scratch[1, n : n + 1, :] = 1.0 / total
        raw = later
    table_ref[0] = scratch[0].T
    table_ref[1] = scratch[1].T


def scored(band, query, keys, rule):
    rows, width = query.shape[1:]
    heads = width // HEAD
    return pl.pallas_call(
        functools.partial(score_kernel, rule),
        in_specs=[SMEM] + [VMEM] * (1 + len(keys)),
        out_specs=[VMEM] * 2,
        out_shape=[
            jax.ShapeDtypeStruct((heads, rows, rows), jnp.bfloat16),
            jax.ShapeDtypeStruct((2, rows, HEAD), jnp.float32),
        ],
        scratch_shapes=[pltpu.VMEM((2, HEAD, rows), jnp.float32)],
        compiler_params=GRANT,
        cost_estimate=pl.CostEstimate(
            flops=2 * rows * rows * width,
            bytes_accessed=6 * rows * width,
            transcendentals=rows * rows * heads,
        ),
    )(band, query, *keys)


def blend_kernel(shares_of, groups, heads, rule, band_ref, weight_ref, table_ref, *refs):
    values, refs = grouped(refs[: sum(shares_of)], shares_of), refs[sum(shares_of) :]
    count = sum(len(group) for group in groups)
    pieces, out_ref = refs[:count], refs[count]
    keeps = kept(rule, band_ref, None)
    rows = out_ref.shape[1]
    lane = lax.broadcasted_iota(jnp.int32, (rows, HEAD), 1)
    value_at = [(value, n) for value in values for n in range(value[0].shape[2] // HEAD)]
    logs = [table_ref[0]]
    places = []
    at = 0
    for keep, group in zip(keeps, groups):
        log = None
        place = []
        for size in group:
            part = read_log(pieces[at], size)
            if log is None:
                log = part
            else:
                log = jnp.where(lane >= len(place), pltpu.roll(part, len(place), 1), log)
            place += [(at, n) for n in range(size)]
            at += 1
        logs.append(log if keep is True else jnp.where(keep, log, NEG))
        places.append(place)
    weights, log = shares(logs)
    coef = weights[0] * table_ref[1]
    if values:
        own_table = packed(coef)
        out_ref[0, :, column(heads)] = log
    else:
        refs[-1][...] = packed(coef)
    tables = [packed(weight) for weight in weights[1:]]
    for n in range(heads):
        out = 0.0
        if values:
            value, index = value_at[n]
            summed = jnp.dot(
                weight_ref[n],
                sum(ref[0, :, column(index)] for ref in value),
                preferred_element_type=jnp.float32,
            )
            out = summed * spread(own_table, n)
        for table, place in zip(tables, places):
            piece, index = place[n]
            block = pieces[piece][0, :, column(index)].astype(jnp.float32)
            out = out + spread(table, n) * block
        out_ref[0, :, column(n)] = out


def blended(band, score, values, groups, rule):
    weights, table = score
    heads, rows = weights.shape[:2]
    width = heads * HEAD
    sizes = tuple(tuple(piece.shape[2] // HEAD - 1 for piece in group) for group in groups)
    pieces = [piece for group in groups for piece in group]
    out_shape = jax.ShapeDtypeStruct((1, rows, width + (HEAD if values else 0)), jnp.float32)
    coef = jax.ShapeDtypeStruct((rows, HEAD), jnp.bfloat16)
    shares_of = tuple(len(value) for value in values)
    flat = [piece for value in values for piece in value]
    if not values:
        weights = table
    out = pl.pallas_call(
        functools.partial(blend_kernel, shares_of, sizes, heads, rule),
        in_specs=[SMEM] + [VMEM] * (2 + len(flat) + len(pieces)),
        out_specs=[VMEM] if values else [VMEM, VMEM],
        out_shape=[out_shape] if values else [out_shape, coef],
        compiler_params=GRANT,
        cost_estimate=pl.CostEstimate(
            flops=2 * rows * rows * width,
            bytes_accessed=2 * rows * width * (len(pieces) + 4),
            transcendentals=0,
        ),
    )(band, weights, table, *flat, *pieces)
    return out[0] if values else out


def final_kernel(first, heads, weight_ref, coef_ref, value_ref, base_ref, *refs):
    out_ref, scratch, sems = refs[-3:]
    copies = []
    for n in range(heads):
        cols = column(first + n)
        summed = jnp.dot(
            weight_ref[first + n],
            value_ref[0, :, column(n)],
            preferred_element_type=jnp.float32,
        )
        out = summed * spread(coef_ref[...], first + n) + base_ref[0, :, cols]
        scratch[:, column(n)] = out.astype(scratch.dtype)
        if (n + 1) % BATCH == 0 or n + 1 == heads:
            start = n // BATCH * BATCH
            done = slice(start * HEAD, (n + 1) * HEAD)
            target = slice((first + start) * HEAD, (first + n + 1) * HEAD)
            copy = pltpu.make_async_copy(
                scratch.at[:, done], out_ref.at[0, :, target], sems.at[n // BATCH]
            )
            copy.start()
            copies.append(copy)
    for copy in copies:
        copy.wait()


def finished(weights, coef, value, base, whole, first):
    rows, width = base.shape[1:]
    heads = value.shape[2] // HEAD
    return pl.pallas_call(
        functools.partial(final_kernel, first, heads),
        in_specs=[VMEM] * 4 + [HBM] * (whole is not None),
        out_specs=HBM,
        out_shape=jax.ShapeDtypeStruct((1, rows, width), value.dtype),
        scratch_shapes=[
            pltpu.VMEM((rows, heads * HEAD), value.dtype),
            pltpu.SemaphoreType.DMA((-(-heads // BATCH),)),
        ],
        input_output_aliases={4: 0} if whole is not None else {},
        compiler_params=GRANT,
        cost_estimate=pl.CostEstimate(
            flops=2 * rows * rows * heads * HEAD,
            bytes_accessed=8 * rows * heads * HEAD,
            transcendentals=0,
        ),
    )(weights, coef, value, base, *([] if whole is None else [whole]))


def per_device(queries, keys, values, band):
    frames, bands = lax.axis_size("frame"), lax.axis_size("row")
    toward = [(f, (f + 2) % frames) if f % 2 else (f, (f - 2) % frames) for f in range(frames)]
    away = [(target, source) for source, target in toward]
    twin = [(f, f ^ 1) for f in range(frames)]
    even = [(r, r ^ 1) for r in range(bands)]
    odd = [(r, r + 1) for r in range(1, bands - 1, 2)]
    odd += [(target, source) for source, target in odd]

    narrow, full = jnp.bfloat16, jnp.float32
    heads = queries.shape[2] // HEAD
    half = heads // 2
    spans = [(0, half), (half, heads - half)]

    cuts = [slice(first * HEAD, (first + size) * HEAD) for first, size in spans]
    value_halves = [values[:, :, cut] for cut in cuts]
    tail = (heads - half) // 5 * 2
    ends = [0, half, heads - tail, heads]
    value_thirds = value_halves[:1] + [
        values[:, :, start * HEAD : stop * HEAD] for start, stop in zip(ends[1:], ends[2:])
    ]
    beyond = [(a, b) for a, b in toward if abs(a - b) != 2]
    within = [(a, b) for a, b in toward if abs(a - b) == 2]

    key_one = lax.ppermute(keys, "frame", toward)
    value_one = [
        (lax.ppermute(value_halves[0], "frame", toward),),
        (
            lax.ppermute(value_halves[1], "frame", within),
            lax.ppermute(value_halves[1], "frame", beyond),
        ),
    ]
    key_two = lax.ppermute(keys, "frame", away)
    value_two = [lax.ppermute(piece, "frame", away) for piece in value_thirds]
    query_twin = []
    for cut in cuts:
        query_twin.append(lax.ppermute(queries[:, :, cut], "frame", twin))
    band_twin = lax.ppermute(band, "frame", twin)
    query_even = lax.ppermute(queries, "row", even)
    query_odd = lax.ppermute(queries, "row", odd)
    twin_even = [lax.ppermute(query_twin[span], "row", even) for span in (0, 1)]
    twin_odd = [lax.ppermute(query_twin[span], "row", odd) for span in (0, 1)]

    def beside_rule(own, other, odd_frame, has_odd):
        return [[own[2] >= 1], [own[2] >= 1], [True]]

    even_part, odd_part, own_part = parts(
        (band, band),
        [query_even, query_odd, queries],
        [keys],
        [(values,)],
        beside_rule,
        (narrow, narrow, full),
        0,
        heads,
    )
    from_even = lax.ppermute(even_part, "row", even)
    from_odd = lax.ppermute(odd_part, "row", odd)

    def twin_rule(own, other, odd_frame, has_odd):
        here = jnp.where(odd_frame, other[3], other[1])
        there = jnp.where(odd_frame, other[1], other[3])
        beside = [here >= 1, there >= 1]
        return [beside, beside, [here >= 0, there >= 0]]

    from_twin = []
    for span, (first, size) in enumerate(spans):
        even_twin, odd_twin, own_twin = parts(
            (band, band_twin),
            [twin_even[span], twin_odd[span], query_twin[span]],
            [keys, key_one],
            [(values,), value_one[span]],
            twin_rule,
            (narrow, narrow, full),
            first,
            size,
        )
        back_even = lax.ppermute(even_twin, "row", even)
        back_odd = lax.ppermute(odd_twin, "row", odd)
        whole = merged(
            band,
            [own_twin, back_even, back_odd],
            lambda own, other, odd_frame, has_odd: [True, True, has_odd],
        )
        from_twin.append(lax.ppermute(whole, "frame", twin))

    near_score = scored(
        band,
        queries,
        [key_one],
        lambda own, other, odd_frame, has_odd: [jnp.where(odd_frame, own[0], own[4]) >= 0],
    )
    near = blended(
        band,
        near_score,
        value_one,
        [[own_part], [from_even], [from_odd]],
        lambda own, other, odd_frame, has_odd: [True, True, has_odd],
    )
    far_score = scored(
        band,
        queries,
        [key_two],
        lambda own, other, odd_frame, has_odd: [jnp.where(odd_frame, own[4], own[0]) >= 0],
    )
    base, coef = blended(
        band,
        far_score,
        [],
        [[near], from_twin],
        lambda own, other, odd_frame, has_odd: [True, True],
    )
    out = None
    for at, first in enumerate(ends[:-1]):
        out = finished(far_score[0], coef, value_two[at], base, out, first)
    return out


def solution(mesh):
    return jax.shard_map(
        per_device,
        mesh=mesh,
        in_specs=(
            P("frame", "row", None),
            P("frame", "row", None),
            P("frame", "row", None),
            P("frame", None),
        ),
        out_specs=P("frame", "row", None),
        check_vma=False,
    )
```

```python
import functools

import jax
import jax.numpy as jnp
from jax import lax
from jax.experimental import pallas as pl
from jax.experimental.pallas import tpu as pltpu
from jax.sharding import PartitionSpec as P


HEAD = 128
NEG = -1e30
RATE = HEAD ** (-0.5) * 1.4426950408889634
THIRD = 32
BATCH = 5
VMEM = pl.BlockSpec(memory_space=pltpu.VMEM)
SMEM = pl.BlockSpec(memory_space=pltpu.SMEM)
HBM = pl.BlockSpec(memory_space=pltpu.HBM)
GRANT = pltpu.CompilerParams(vmem_limit_bytes=16 << 20)


def column(index):
    return slice(index * HEAD, (index + 1) * HEAD)


def raw_scores(key, query):
    return lax.dot_general(
        key, query, (((1,), (1,)), ((), ())), preferred_element_type=jnp.float32
    )


def weighted(value, weights):
    return lax.dot_general(
        value, weights, (((0,), (0,)), ((), ())), preferred_element_type=jnp.float32
    )


def softmax_rows(raw):
    largest = functools.reduce(
        jnp.maximum, [jnp.max(part, axis=0, keepdims=True) for part in raw]
    )
    expos = [jnp.exp2((part - largest) * RATE) for part in raw]
    total = sum(jnp.sum(expo, axis=0, keepdims=True) for expo in expos)
    return [expo.astype(jnp.bfloat16) for expo in expos], total, largest


def thirds(value):
    high = value.astype(jnp.bfloat16).astype(jnp.float32)
    middle = (value - high).astype(jnp.bfloat16).astype(jnp.float32)
    return high, middle, value - high - middle


def packed(value):
    lane = lax.broadcasted_iota(jnp.int32, value.shape, 1)
    high, middle, low = thirds(value)
    rest = jnp.where(
        lane < 2 * THIRD, pltpu.roll(middle, THIRD, 1), pltpu.roll(low, 2 * THIRD, 1)
    )
    return jnp.where(lane < THIRD, high, rest).astype(jnp.bfloat16)


def read_log(block, heads):
    log = block[0, :, column(heads)].astype(jnp.float32)
    if block.dtype == jnp.float32:
        return log
    return log + pltpu.roll(log, HEAD - THIRD, 1) + pltpu.roll(log, HEAD - 2 * THIRD, 1)


def spread(table, n):
    row = lax.broadcasted_iota(jnp.int32, (HEAD, HEAD), 0)
    chosen = (row == n) | (row == THIRD + n) | (row == 2 * THIRD + n)
    return jnp.dot(
        table,
        jnp.where(chosen, 1.0, 0.0).astype(jnp.bfloat16),
        preferred_element_type=jnp.float32,
    )


def shares(logs):
    largest = functools.reduce(jnp.maximum, logs)
    expos = [jnp.exp2(log - largest) for log in logs]
    total = sum(expos)
    inverse = 1.0 / total
    return [expo * inverse for expo in expos], largest + jnp.log2(total)


def kept(rule, band_ref, twin_ref):
    odd_frame = lax.axis_index("frame") % 2 == 1
    row = lax.axis_index("row")
    return rule(
        [band_ref[0, i] for i in range(5)],
        [twin_ref[0, i] for i in range(5)] if twin_ref is not None else None,
        odd_frame,
        (row > 0) & (row < lax.axis_size("row") - 1),
    )


def grouped(refs, sizes):
    groups, at = [], 0
    for size in sizes:
        groups.append(refs[at : at + size])
        at += size
    return groups


def parts_kernel(query_count, key_count, shares_of, first, heads, rule, *refs):
    band_ref, twin_ref, refs = refs[0], refs[1], refs[2:]
    queries = refs[:query_count]
    keys = refs[query_count : query_count + key_count]
    values = grouped(refs[query_count + key_count : query_count + key_count + sum(shares_of)], shares_of)
    outs = refs[query_count + key_count + sum(shares_of) : -1]
    log_scratch = refs[-1]
    rows = queries[0].shape[1]
    wide = query_count * rows
    lane = lax.broadcasted_iota(jnp.int32, (1, wide), 1)
    keeps = kept(rule, band_ref, twin_ref)
    biases = []
    for i in range(key_count):
        bias = jnp.zeros((1, wide), jnp.float32)
        for at in range(query_count):
            if keeps[at][i] is not True:
                bias = jnp.where(
                    (lane >= at * rows) & (lane < (at + 1) * rows),
                    jnp.where(keeps[at][i], 0.0, NEG),
                    bias,
                )
        biases.append(bias)
    log_scratch[...] = jnp.zeros(log_scratch.shape, jnp.float32)

    def of(ref, n):
        start = 0 if ref.shape[2] == heads * HEAD else first
        return ref[0, :, column(start + n)]

    def score(n):
        query = jnp.concatenate([of(ref, n) for ref in queries], 0)
        return [raw_scores(of(key, n), query) + bias for key, bias in zip(keys, biases)]

    def attend(n, weights, total, largest):
        summed = sum(
            weighted(sum(of(ref, n) for ref in value), part)
            for value, part in zip(values, weights)
        )
        log_scratch[n : n + 1, :] = largest * RATE + jnp.log2(total)
        normed = (summed * (1.0 / total)).T
        for at, out in enumerate(outs):
            out[0, :, column(n)] = normed[at * rows : (at + 1) * rows].astype(out.dtype)

    raw = score(0)
    before = None
    for n in range(heads):
        later = score(n + 1) if n + 1 < heads else None
        now = softmax_rows(raw)
        if before is not None:
            attend(n - 1, *before)
        before, raw = now, later
    attend(heads - 1, *before)
    logs = log_scratch[...].T
    for at, out in enumerate(outs):
        log = logs[at * rows : (at + 1) * rows]
        out[0, :, column(heads)] = log if out.dtype == jnp.float32 else packed(log)


def parts(bands, queries, keys, values, rule, kinds, first, heads):
    rows = queries[0].shape[1]
    wide = len(queries) * rows
    blocks = len(queries) * len(keys)
    width = heads * HEAD
    shares_of = tuple(len(value) for value in values)
    flat = [piece for value in values for piece in value]
    return pl.pallas_call(
        functools.partial(
            parts_kernel, len(queries), len(keys), shares_of, first, heads, rule
        ),
        in_specs=[SMEM] * 2 + [VMEM] * (len(queries) + len(keys) + len(flat)),
        out_specs=[VMEM] * len(queries),
        out_shape=[
            jax.ShapeDtypeStruct((1, rows, width + HEAD), kind) for kind in kinds
        ],
        scratch_shapes=[pltpu.VMEM((HEAD, wide), jnp.float32)],
        compiler_params=GRANT,
        cost_estimate=pl.CostEstimate(
            flops=4 * rows * rows * width * blocks,
            bytes_accessed=2 * rows * width * (2 * len(queries) + 2 * len(keys)),
            transcendentals=rows * rows * heads * blocks,
        ),
    )(*bands, *queries, *keys, *flat)


def merge_kernel(heads, rule, band_ref, *refs):
    blocks, out_ref = refs[:-1], refs[-1]
    keeps = kept(rule, band_ref, None)
    logs = []
    for keep, block in zip(keeps, blocks):
        log = read_log(block, heads)
        logs.append(log if keep is True else jnp.where(keep, log, NEG))
    weights, log = shares(logs)
    tables = [packed(weight) for weight in weights]
    for n in range(heads):
        cols = column(n)
        out_ref[0, :, cols] = sum(
            spread(table, n) * block[0, :, cols].astype(jnp.float32)
            for table, block in zip(tables, blocks)
        ).astype(out_ref.dtype)
    out_ref[0, :, column(heads)] = packed(log)


def merged(band, blocks, rule):
    rows, width = blocks[0].shape[1:]
    heads = width // HEAD - 1
    return pl.pallas_call(
        functools.partial(merge_kernel, heads, rule),
        in_specs=[SMEM] + [VMEM] * len(blocks),
        out_specs=VMEM,
        out_shape=jax.ShapeDtypeStruct((1, rows, width), jnp.bfloat16),
        compiler_params=GRANT,
        cost_estimate=pl.CostEstimate(
            flops=2 * rows * width * len(blocks),
            bytes_accessed=2 * rows * width * (len(blocks) + 1),
            transcendentals=0,
        ),
    )(band, *blocks)


def score_kernel(heads, rule, band_ref, query_ref, *refs):
    keys, (weight_ref, table_ref, scratch) = refs[:-3], refs[-3:]
    biases = [
        None if keep is True else jnp.where(keep, 0.0, NEG)
        for keep in kept(rule, band_ref, None)
    ]
    scratch[...] = jnp.zeros(scratch.shape, jnp.float32)

    def score(n):
        cols = column(n)
        parts = [raw_scores(key[0, :, cols], query_ref[0, :, cols]) for key in keys]
        return [part if bias is None else part + bias for part, bias in zip(parts, biases)]

    raw = score(0)
    for n in range(heads):
        later = score(n + 1) if n + 1 < heads else None
        weights, total, largest = softmax_rows(raw)
        for at, weight in enumerate(weights):
            weight_ref[at, n] = weight.T
        scratch[0, n : n + 1, :] = largest * RATE + jnp.log2(total)
        scratch[1, n : n + 1, :] = 1.0 / total
        raw = later
    table_ref[0] = scratch[0].T
    table_ref[1] = scratch[1].T


def scored(band, query, keys, rule):
    rows, width = query.shape[1:]
    heads = width // HEAD
    return pl.pallas_call(
        functools.partial(score_kernel, heads, rule),
        in_specs=[SMEM] + [VMEM] * (1 + len(keys)),
        out_specs=[VMEM] * 2,
        out_shape=[
            jax.ShapeDtypeStruct((len(keys), heads, rows, rows), jnp.bfloat16),
            jax.ShapeDtypeStruct((2, rows, HEAD), jnp.float32),
        ],
        scratch_shapes=[pltpu.VMEM((2, HEAD, rows), jnp.float32)],
        compiler_params=GRANT,
        cost_estimate=pl.CostEstimate(
            flops=2 * rows * rows * width * len(keys),
            bytes_accessed=6 * rows * width,
            transcendentals=rows * rows * heads * len(keys),
        ),
    )(band, query, *keys)


def near_kernel(shares_of, sources, heads, weight_ref, table_ref, *refs):
    pieces, out_ref = grouped(refs[:-1], shares_of), refs[-1]
    table = packed(table_ref[1])
    for n in range(heads):
        summed = 0.0
        for at, source in enumerate(sources):
            piece, index = source[n]
            value = sum(ref[0, :, column(index)] for ref in pieces[piece])
            summed = summed + jnp.dot(
                weight_ref[at, n], value, preferred_element_type=jnp.float32
            )
        out_ref[0, :, column(n)] = summed * spread(table, n)
    out_ref[0, :, column(heads)] = table_ref[0]


def neared(score, values):
    weights, table = score
    heads, rows = weights.shape[1:3]
    sources, pieces = [], []
    for value in values:
        source = []
        for piece in value:
            size = piece[0].shape[2] // HEAD
            source += [(len(pieces), n) for n in range(size)]
            pieces.append(piece)
        sources.append(tuple(source))
    flat = [ref for piece in pieces for ref in piece]
    width = heads * HEAD
    return pl.pallas_call(
        functools.partial(
            near_kernel, tuple(len(piece) for piece in pieces), tuple(sources), heads
        ),
        in_specs=[VMEM] * (2 + len(flat)),
        out_specs=VMEM,
        out_shape=jax.ShapeDtypeStruct((1, rows, width + HEAD), jnp.float32),
        compiler_params=GRANT,
        cost_estimate=pl.CostEstimate(
            flops=2 * rows * rows * width * len(values),
            bytes_accessed=2 * rows * width * (len(values) + 4),
            transcendentals=0,
        ),
    )(weights, table, *flat)


def base_kernel(sizes, heads, table_ref, near_ref, *refs):
    pieces, (out_ref, coef_ref) = refs[: len(sizes)], refs[len(sizes) :]
    lane = lax.broadcasted_iota(jnp.int32, (out_ref.shape[1], HEAD), 1)
    log, place = None, []
    for at, (piece, size) in enumerate(zip(pieces, sizes)):
        part = read_log(piece, size)
        if at:
            part = jnp.where(lane >= len(place), pltpu.roll(part, len(place), 1), log)
        log = part
        place += [(at, n) for n in range(size)]
    weights, _ = shares([table_ref[0], read_log(near_ref, heads), log])
    coef_ref[...] = packed(weights[0] * table_ref[1])
    near_table, twin_table = packed(weights[1]), packed(weights[2])
    for n in range(heads):
        piece, index = place[n]
        block = pieces[piece][0, :, column(index)].astype(jnp.float32)
        out_ref[0, :, column(n)] = (
            spread(near_table, n) * near_ref[0, :, column(n)] + spread(twin_table, n) * block
        )


def based(score, near, pieces):
    table = score[1]
    rows = near.shape[1]
    heads = near.shape[2] // HEAD - 1
    sizes = tuple(piece.shape[2] // HEAD - 1 for piece in pieces)
    return pl.pallas_call(
        functools.partial(base_kernel, sizes, heads),
        in_specs=[VMEM] * (2 + len(pieces)),
        out_specs=[VMEM, VMEM],
        out_shape=[
            jax.ShapeDtypeStruct((1, rows, heads * HEAD), jnp.float32),
            jax.ShapeDtypeStruct((rows, HEAD), jnp.bfloat16),
        ],
        compiler_params=GRANT,
        cost_estimate=pl.CostEstimate(
            flops=4 * rows * heads * HEAD,
            bytes_accessed=12 * rows * heads * HEAD,
            transcendentals=0,
        ),
    )(table, near, *pieces)


def final_kernel(first, heads, weight_ref, coef_ref, value_ref, base_ref, *refs):
    out_ref, scratch, sems = refs[-3:]
    copies = []
    for n in range(heads):
        cols = column(first + n)
        summed = jnp.dot(
            weight_ref[0, first + n],
            value_ref[0, :, column(n)],
            preferred_element_type=jnp.float32,
        )
        out = summed * spread(coef_ref[...], first + n) + base_ref[0, :, cols]
        scratch[:, column(n)] = out.astype(scratch.dtype)
        if (n + 1) % BATCH == 0 or n + 1 == heads:
            start = n // BATCH * BATCH
            done = slice(start * HEAD, (n + 1) * HEAD)
            target = slice((first + start) * HEAD, (first + n + 1) * HEAD)
            copy = pltpu.make_async_copy(
                scratch.at[:, done], out_ref.at[0, :, target], sems.at[n // BATCH]
            )
            copy.start()
            copies.append(copy)
    for copy in copies:
        copy.wait()


def finished(weights, coef, value, base, whole, first):
    rows, width = base.shape[1:]
    heads = value.shape[2] // HEAD
    return pl.pallas_call(
        functools.partial(final_kernel, first, heads),
        in_specs=[VMEM] * 4 + [HBM] * (whole is not None),
        out_specs=HBM,
        out_shape=jax.ShapeDtypeStruct((1, rows, width), value.dtype),
        scratch_shapes=[
            pltpu.VMEM((rows, heads * HEAD), value.dtype),
            pltpu.SemaphoreType.DMA((-(-heads // BATCH),)),
        ],
        input_output_aliases={4: 0} if whole is not None else {},
        compiler_params=GRANT,
        cost_estimate=pl.CostEstimate(
            flops=2 * rows * rows * heads * HEAD,
            bytes_accessed=8 * rows * heads * HEAD,
            transcendentals=0,
        ),
    )(weights, coef, value, base, *([] if whole is None else [whole]))


def per_device(queries, keys, values, band):
    frames, bands = lax.axis_size("frame"), lax.axis_size("row")
    toward = [(f, (f + 2) % frames) if f % 2 else (f, (f - 2) % frames) for f in range(frames)]
    away = [(target, source) for source, target in toward]
    twin = [(f, f ^ 1) for f in range(frames)]
    even = [(r, r ^ 1) for r in range(bands)]
    odd = [(r, r + 1) for r in range(1, bands - 1, 2)]
    odd += [(target, source) for source, target in odd]

    narrow, full = jnp.bfloat16, jnp.float32
    heads = queries.shape[2] // HEAD
    half = heads // 2
    spans = [(0, half), (half, heads - half)]

    cuts = [slice(first * HEAD, (first + size) * HEAD) for first, size in spans]
    value_halves = [values[:, :, cut] for cut in cuts]
    tail = (heads - half) // 5 * 2
    ends = [0, half, heads - tail, heads]
    value_thirds = value_halves[:1] + [
        values[:, :, start * HEAD : stop * HEAD] for start, stop in zip(ends[1:], ends[2:])
    ]
    beyond = [(a, b) for a, b in toward if abs(a - b) != 2]
    within = [(a, b) for a, b in toward if abs(a - b) == 2]

    key_one = lax.ppermute(keys, "frame", toward)
    value_one = [
        (lax.ppermute(value_halves[0], "frame", toward),),
        (
            lax.ppermute(value_halves[1], "frame", within),
            lax.ppermute(value_halves[1], "frame", beyond),
        ),
    ]
    key_two = lax.ppermute(keys, "frame", away)
    value_two = [lax.ppermute(piece, "frame", away) for piece in value_thirds]
    query_twin = []
    for cut in cuts:
        query_twin.append(lax.ppermute(queries[:, :, cut], "frame", twin))
    band_twin = lax.ppermute(band, "frame", twin)
    key_even = lax.ppermute(keys, "row", even)
    key_odd = lax.ppermute(keys, "row", odd)
    value_even = lax.ppermute(values, "row", even)
    value_odd = lax.ppermute(values, "row", odd)
    twin_even = [lax.ppermute(query_twin[span], "row", even) for span in (0, 1)]
    twin_odd = [lax.ppermute(query_twin[span], "row", odd) for span in (0, 1)]

    def twin_rule(own, other, odd_frame, has_odd):
        here = jnp.where(odd_frame, other[3], other[1])
        there = jnp.where(odd_frame, other[1], other[3])
        beside = [here >= 1, there >= 1]
        return [beside, beside, [here >= 0, there >= 0]]

    from_twin = []
    for span, (first, size) in enumerate(spans):
        even_twin, odd_twin, own_twin = parts(
            (band, band_twin),
            [twin_even[span], twin_odd[span], query_twin[span]],
            [keys, key_one],
            [(values,), value_one[span]],
            twin_rule,
            (narrow, narrow, full),
            first,
            size,
        )
        back_even = lax.ppermute(even_twin, "row", even)
        back_odd = lax.ppermute(odd_twin, "row", odd)
        whole = merged(
            band,
            [own_twin, back_even, back_odd],
            lambda own, other, odd_frame, has_odd: [True, True, has_odd],
        )
        from_twin.append(lax.ppermute(whole, "frame", twin))

    def near_rule(own, other, odd_frame, has_odd):
        beside = own[2] >= 1
        return [True, jnp.where(odd_frame, own[0], own[4]) >= 0, beside, beside & has_odd]

    near_score = scored(band, queries, [keys, key_one, key_even, key_odd], near_rule)
    near = neared(near_score, [[(values,)], value_one, [(value_even,)], [(value_odd,)]])
    far_score = scored(
        band,
        queries,
        [key_two],
        lambda own, other, odd_frame, has_odd: [jnp.where(odd_frame, own[4], own[0]) >= 0],
    )
    base, coef = based(far_score, near, from_twin)
    out = None
    for at, first in enumerate(ends[:-1]):
        out = finished(far_score[0], coef, value_two[at], base, out, first)
    return out


def solution(mesh):
    return jax.shard_map(
        per_device,
        mesh=mesh,
        in_specs=(
            P("frame", "row", None),
            P("frame", "row", None),
            P("frame", "row", None),
            P("frame", None),
        ),
        out_specs=P("frame", "row", None),
        check_vma=False,
    )
```

```python
import functools

import jax
import jax.numpy as jnp
from jax import lax
from jax.experimental import pallas as pl
from jax.experimental.pallas import tpu as pltpu
from jax.sharding import PartitionSpec as P


HEAD = 128
NEG = -1e30
RATE = HEAD ** (-0.5) * 1.4426950408889634
THIRD = 32
BATCH = 5
VMEM = pl.BlockSpec(memory_space=pltpu.VMEM)
SMEM = pl.BlockSpec(memory_space=pltpu.SMEM)
HBM = pl.BlockSpec(memory_space=pltpu.HBM)
GRANT = pltpu.CompilerParams(vmem_limit_bytes=16 << 20)


def column(index):
    return slice(index * HEAD, (index + 1) * HEAD)


def raw_scores(key, query):
    return lax.dot_general(
        key, query, (((1,), (1,)), ((), ())), preferred_element_type=jnp.float32
    )


def weighted(value, weights):
    return lax.dot_general(
        value, weights, (((0,), (0,)), ((), ())), preferred_element_type=jnp.float32
    )


def softmax_rows(raw):
    largest = functools.reduce(
        jnp.maximum, [jnp.max(part, axis=0, keepdims=True) for part in raw]
    )
    expos = [jnp.exp2((part - largest) * RATE) for part in raw]
    total = sum(jnp.sum(expo, axis=0, keepdims=True) for expo in expos)
    return [expo.astype(jnp.bfloat16) for expo in expos], total, largest


def thirds(value):
    high = value.astype(jnp.bfloat16).astype(jnp.float32)
    middle = (value - high).astype(jnp.bfloat16).astype(jnp.float32)
    return high, middle, value - high - middle


def packed(value):
    lane = lax.broadcasted_iota(jnp.int32, value.shape, 1)
    high, middle, low = thirds(value)
    rest = jnp.where(
        lane < 2 * THIRD, pltpu.roll(middle, THIRD, 1), pltpu.roll(low, 2 * THIRD, 1)
    )
    return jnp.where(lane < THIRD, high, rest).astype(jnp.bfloat16)


def read_log(block, heads):
    log = block[0, :, column(heads)].astype(jnp.float32)
    if block.dtype == jnp.float32:
        return log
    return log + pltpu.roll(log, HEAD - THIRD, 1) + pltpu.roll(log, HEAD - 2 * THIRD, 1)


def spread(table, n):
    row = lax.broadcasted_iota(jnp.int32, (HEAD, HEAD), 0)
    chosen = (row == n) | (row == THIRD + n) | (row == 2 * THIRD + n)
    return jnp.dot(
        table,
        jnp.where(chosen, 1.0, 0.0).astype(jnp.bfloat16),
        preferred_element_type=jnp.float32,
    )


def shares(logs):
    largest = functools.reduce(jnp.maximum, logs)
    expos = [jnp.exp2(log - largest) for log in logs]
    total = sum(expos)
    inverse = 1.0 / total
    return [expo * inverse for expo in expos], largest + jnp.log2(total)


def kept(rule, band_ref, twin_ref):
    odd_frame = lax.axis_index("frame") % 2 == 1
    row = lax.axis_index("row")
    return rule(
        [band_ref[0, i] for i in range(5)],
        [twin_ref[0, i] for i in range(5)] if twin_ref is not None else None,
        odd_frame,
        (row > 0) & (row < lax.axis_size("row") - 1),
    )


def grouped(refs, sizes):
    groups, at = [], 0
    for size in sizes:
        groups.append(refs[at : at + size])
        at += size
    return groups


def parts_kernel(query_count, key_count, shares_of, first, heads, rule, *refs):
    band_ref, twin_ref, refs = refs[0], refs[1], refs[2:]
    queries = refs[:query_count]
    keys = refs[query_count : query_count + key_count]
    values = grouped(refs[query_count + key_count : query_count + key_count + sum(shares_of)], shares_of)
    outs = refs[query_count + key_count + sum(shares_of) : -1]
    log_scratch = refs[-1]
    rows = queries[0].shape[1]
    wide = query_count * rows
    lane = lax.broadcasted_iota(jnp.int32, (1, wide), 1)
    keeps = kept(rule, band_ref, twin_ref)
    biases = []
    for i in range(key_count):
        bias = jnp.zeros((1, wide), jnp.float32)
        for at in range(query_count):
            if keeps[at][i] is not True:
                bias = jnp.where(
                    (lane >= at * rows) & (lane < (at + 1) * rows),
                    jnp.where(keeps[at][i], 0.0, NEG),
                    bias,
                )
        biases.append(bias)
    log_scratch[...] = jnp.zeros(log_scratch.shape, jnp.float32)

    def of(ref, n):
        start = 0 if ref.shape[2] == heads * HEAD else first
        return ref[0, :, column(start + n)]

    def score(n):
        query = jnp.concatenate([of(ref, n) for ref in queries], 0)
        return [raw_scores(of(key, n), query) + bias for key, bias in zip(keys, biases)]

    def attend(n, weights, total, largest):
        summed = sum(
            weighted(sum(of(ref, n) for ref in value), part)
            for value, part in zip(values, weights)
        )
        log_scratch[n : n + 1, :] = largest * RATE + jnp.log2(total)
        normed = (summed * (1.0 / total)).T
        for at, out in enumerate(outs):
            out[0, :, column(n)] = normed[at * rows : (at + 1) * rows].astype(out.dtype)

    raw = score(0)
    before = None
    for n in range(heads):
        later = score(n + 1) if n + 1 < heads else None
        now = softmax_rows(raw)
        if before is not None:
            attend(n - 1, *before)
        before, raw = now, later
    attend(heads - 1, *before)
    logs = log_scratch[...].T
    for at, out in enumerate(outs):
        log = logs[at * rows : (at + 1) * rows]
        out[0, :, column(heads)] = log if out.dtype == jnp.float32 else packed(log)


def parts(bands, queries, keys, values, rule, kinds, first, heads):
    rows = queries[0].shape[1]
    wide = len(queries) * rows
    blocks = len(queries) * len(keys)
    width = heads * HEAD
    shares_of = tuple(len(value) for value in values)
    flat = [piece for value in values for piece in value]
    return pl.pallas_call(
        functools.partial(
            parts_kernel, len(queries), len(keys), shares_of, first, heads, rule
        ),
        in_specs=[SMEM] * 2 + [VMEM] * (len(queries) + len(keys) + len(flat)),
        out_specs=[VMEM] * len(queries),
        out_shape=[
            jax.ShapeDtypeStruct((1, rows, width + HEAD), kind) for kind in kinds
        ],
        scratch_shapes=[pltpu.VMEM((HEAD, wide), jnp.float32)],
        compiler_params=GRANT,
        cost_estimate=pl.CostEstimate(
            flops=4 * rows * rows * width * blocks,
            bytes_accessed=2 * rows * width * (2 * len(queries) + 2 * len(keys)),
            transcendentals=rows * rows * heads * blocks,
        ),
    )(*bands, *queries, *keys, *flat)


def merge_kernel(heads, rule, band_ref, *refs):
    blocks, out_ref = refs[:-1], refs[-1]
    keeps = kept(rule, band_ref, None)
    logs = []
    for keep, block in zip(keeps, blocks):
        log = read_log(block, heads)
        logs.append(log if keep is True else jnp.where(keep, log, NEG))
    weights, log = shares(logs)
    tables = [packed(weight) for weight in weights]
    for n in range(heads):
        cols = column(n)
        out_ref[0, :, cols] = sum(
            spread(table, n) * block[0, :, cols].astype(jnp.float32)
            for table, block in zip(tables, blocks)
        ).astype(out_ref.dtype)
    out_ref[0, :, column(heads)] = packed(log)


def merged(band, blocks, rule):
    rows, width = blocks[0].shape[1:]
    heads = width // HEAD - 1
    return pl.pallas_call(
        functools.partial(merge_kernel, heads, rule),
        in_specs=[SMEM] + [VMEM] * len(blocks),
        out_specs=VMEM,
        out_shape=jax.ShapeDtypeStruct((1, rows, width), jnp.bfloat16),
        compiler_params=GRANT,
        cost_estimate=pl.CostEstimate(
            flops=2 * rows * width * len(blocks),
            bytes_accessed=2 * rows * width * (len(blocks) + 1),
            transcendentals=0,
        ),
    )(band, *blocks)


def score_kernel(heads, rule, band_ref, query_ref, *refs):
    keys, (weight_ref, table_ref, scratch) = refs[:-3], refs[-3:]
    biases = [
        None if keep is True else jnp.where(keep, 0.0, NEG)
        for keep in kept(rule, band_ref, None)
    ]
    scratch[...] = jnp.zeros(scratch.shape, jnp.float32)

    def score(n):
        cols = column(n)
        parts = [raw_scores(key[0, :, cols], query_ref[0, :, cols]) for key in keys]
        return [part if bias is None else part + bias for part, bias in zip(parts, biases)]

    raw = score(0)
    for n in range(heads):
        later = score(n + 1) if n + 1 < heads else None
        weights, total, largest = softmax_rows(raw)
        for at, weight in enumerate(weights):
            weight_ref[at, n] = weight.T
        scratch[0, n : n + 1, :] = largest * RATE + jnp.log2(total)
        scratch[1, n : n + 1, :] = 1.0 / total
        raw = later
    table_ref[0] = scratch[0].T
    table_ref[1] = scratch[1].T


def scored(band, query, keys, rule):
    rows, width = query.shape[1:]
    heads = width // HEAD
    return pl.pallas_call(
        functools.partial(score_kernel, heads, rule),
        in_specs=[SMEM] + [VMEM] * (1 + len(keys)),
        out_specs=[VMEM] * 2,
        out_shape=[
            jax.ShapeDtypeStruct((len(keys), heads, rows, rows), jnp.bfloat16),
            jax.ShapeDtypeStruct((2, rows, HEAD), jnp.float32),
        ],
        scratch_shapes=[pltpu.VMEM((2, HEAD, rows), jnp.float32)],
        compiler_params=GRANT,
        cost_estimate=pl.CostEstimate(
            flops=2 * rows * rows * width * len(keys),
            bytes_accessed=6 * rows * width,
            transcendentals=rows * rows * heads * len(keys),
        ),
    )(band, query, *keys)


def near_kernel(counts, shares_of, sources, heads, *refs):
    size = len(counts)
    weight_refs, table_refs = refs[:size], refs[size : 2 * size]
    pieces, out_ref = grouped(refs[2 * size : -1], shares_of), refs[-1]
    portions, log = shares([table_ref[0] for table_ref in table_refs])
    tables = [
        packed(portion * table_ref[1]) for portion, table_ref in zip(portions, table_refs)
    ]
    for n in range(heads):
        out = 0.0
        at = 0
        for count, weight_ref, table in zip(counts, weight_refs, tables):
            summed = 0.0
            for i in range(count):
                piece, index = sources[at][n]
                value = sum(ref[0, :, column(index)] for ref in pieces[piece])
                summed = summed + jnp.dot(
                    weight_ref[i, n], value, preferred_element_type=jnp.float32
                )
                at += 1
            out = out + summed * spread(table, n)
        out_ref[0, :, column(n)] = out
    out_ref[0, :, column(heads)] = log


def neared(scores, values):
    heads, rows = scores[0][0].shape[1:3]
    counts = tuple(weights.shape[0] for weights, _ in scores)
    sources, pieces = [], []
    for value in values:
        source = []
        for piece in value:
            size = piece[0].shape[2] // HEAD
            source += [(len(pieces), n) for n in range(size)]
            pieces.append(piece)
        sources.append(tuple(source))
    flat = [ref for piece in pieces for ref in piece]
    width = heads * HEAD
    return pl.pallas_call(
        functools.partial(
            near_kernel,
            counts,
            tuple(len(piece) for piece in pieces),
            tuple(sources),
            heads,
        ),
        in_specs=[VMEM] * (2 * len(scores) + len(flat)),
        out_specs=VMEM,
        out_shape=jax.ShapeDtypeStruct((1, rows, width + HEAD), jnp.float32),
        compiler_params=GRANT,
        cost_estimate=pl.CostEstimate(
            flops=2 * rows * rows * width * len(values),
            bytes_accessed=2 * rows * width * (len(values) + 4),
            transcendentals=0,
        ),
    )(*[score[0] for score in scores], *[score[1] for score in scores], *flat)


def base_kernel(sizes, heads, table_ref, near_ref, *refs):
    pieces, (out_ref, coef_ref) = refs[: len(sizes)], refs[len(sizes) :]
    lane = lax.broadcasted_iota(jnp.int32, (out_ref.shape[1], HEAD), 1)
    log, place = None, []
    for at, (piece, size) in enumerate(zip(pieces, sizes)):
        part = read_log(piece, size)
        if at:
            part = jnp.where(lane >= len(place), pltpu.roll(part, len(place), 1), log)
        log = part
        place += [(at, n) for n in range(size)]
    weights, _ = shares([table_ref[0], read_log(near_ref, heads), log])
    coef_ref[...] = packed(weights[0] * table_ref[1])
    near_table, twin_table = packed(weights[1]), packed(weights[2])
    for n in range(heads):
        piece, index = place[n]
        block = pieces[piece][0, :, column(index)].astype(jnp.float32)
        out_ref[0, :, column(n)] = (
            spread(near_table, n) * near_ref[0, :, column(n)] + spread(twin_table, n) * block
        )


def based(score, near, pieces):
    table = score[1]
    rows = near.shape[1]
    heads = near.shape[2] // HEAD - 1
    sizes = tuple(piece.shape[2] // HEAD - 1 for piece in pieces)
    return pl.pallas_call(
        functools.partial(base_kernel, sizes, heads),
        in_specs=[VMEM] * (2 + len(pieces)),
        out_specs=[VMEM, VMEM],
        out_shape=[
            jax.ShapeDtypeStruct((1, rows, heads * HEAD), jnp.float32),
            jax.ShapeDtypeStruct((rows, HEAD), jnp.bfloat16),
        ],
        compiler_params=GRANT,
        cost_estimate=pl.CostEstimate(
            flops=4 * rows * heads * HEAD,
            bytes_accessed=12 * rows * heads * HEAD,
            transcendentals=0,
        ),
    )(table, near, *pieces)


def final_kernel(first, heads, weight_ref, coef_ref, value_ref, base_ref, *refs):
    out_ref, scratch, sems = refs[-3:]
    copies = []
    for n in range(heads):
        cols = column(first + n)
        summed = jnp.dot(
            weight_ref[0, first + n],
            value_ref[0, :, column(n)],
            preferred_element_type=jnp.float32,
        )
        out = summed * spread(coef_ref[...], first + n) + base_ref[0, :, cols]
        scratch[:, column(n)] = out.astype(scratch.dtype)
        if (n + 1) % BATCH == 0 or n + 1 == heads:
            start = n // BATCH * BATCH
            done = slice(start * HEAD, (n + 1) * HEAD)
            target = slice((first + start) * HEAD, (first + n + 1) * HEAD)
            copy = pltpu.make_async_copy(
                scratch.at[:, done], out_ref.at[0, :, target], sems.at[n // BATCH]
            )
            copy.start()
            copies.append(copy)
    for copy in copies:
        copy.wait()


def finished(weights, coef, value, base, whole, first):
    rows, width = base.shape[1:]
    heads = value.shape[2] // HEAD
    return pl.pallas_call(
        functools.partial(final_kernel, first, heads),
        in_specs=[VMEM] * 4 + [HBM] * (whole is not None),
        out_specs=HBM,
        out_shape=jax.ShapeDtypeStruct((1, rows, width), value.dtype),
        scratch_shapes=[
            pltpu.VMEM((rows, heads * HEAD), value.dtype),
            pltpu.SemaphoreType.DMA((-(-heads // BATCH),)),
        ],
        input_output_aliases={4: 0} if whole is not None else {},
        compiler_params=GRANT,
        cost_estimate=pl.CostEstimate(
            flops=2 * rows * rows * heads * HEAD,
            bytes_accessed=8 * rows * heads * HEAD,
            transcendentals=0,
        ),
    )(weights, coef, value, base, *([] if whole is None else [whole]))


def per_device(queries, keys, values, band):
    frames, bands = lax.axis_size("frame"), lax.axis_size("row")
    toward = [(f, (f + 2) % frames) if f % 2 else (f, (f - 2) % frames) for f in range(frames)]
    away = [(target, source) for source, target in toward]
    twin = [(f, f ^ 1) for f in range(frames)]
    even = [(r, r ^ 1) for r in range(bands)]
    odd = [(r, r + 1) for r in range(1, bands - 1, 2)]
    odd += [(target, source) for source, target in odd]

    narrow, full = jnp.bfloat16, jnp.float32
    heads = queries.shape[2] // HEAD
    half = heads // 2
    spans = [(0, half), (half, heads - half)]

    cuts = [slice(first * HEAD, (first + size) * HEAD) for first, size in spans]
    value_halves = [values[:, :, cut] for cut in cuts]
    tail = (heads - half) // 5 * 2
    ends = [0, half, heads - tail, heads]
    value_thirds = value_halves[:1] + [
        values[:, :, start * HEAD : stop * HEAD] for start, stop in zip(ends[1:], ends[2:])
    ]
    beyond = [(a, b) for a, b in toward if abs(a - b) != 2]
    within = [(a, b) for a, b in toward if abs(a - b) == 2]

    key_one = lax.ppermute(keys, "frame", toward)
    value_one = [
        (lax.ppermute(value_halves[0], "frame", toward),),
        (
            lax.ppermute(value_halves[1], "frame", within),
            lax.ppermute(value_halves[1], "frame", beyond),
        ),
    ]
    key_two = lax.ppermute(keys, "frame", away)
    value_two = [lax.ppermute(piece, "frame", away) for piece in value_thirds]
    query_twin = []
    for cut in cuts:
        query_twin.append(lax.ppermute(queries[:, :, cut], "frame", twin))
    band_twin = lax.ppermute(band, "frame", twin)
    key_even = lax.ppermute(keys, "row", even)
    key_odd = lax.ppermute(keys, "row", odd)
    value_even = lax.ppermute(values, "row", even)
    value_odd = lax.ppermute(values, "row", odd)
    twin_even = [lax.ppermute(query_twin[span], "row", even) for span in (0, 1)]
    twin_odd = [lax.ppermute(query_twin[span], "row", odd) for span in (0, 1)]

    def twin_rule(own, other, odd_frame, has_odd):
        here = jnp.where(odd_frame, other[3], other[1])
        there = jnp.where(odd_frame, other[1], other[3])
        beside = [here >= 1, there >= 1]
        return [beside, beside, [here >= 0, there >= 0]]

    from_twin = []
    for span, (first, size) in enumerate(spans):
        even_twin, odd_twin, own_twin = parts(
            (band, band_twin),
            [twin_even[span], twin_odd[span], query_twin[span]],
            [keys, key_one],
            [(values,), value_one[span]],
            twin_rule,
            (narrow, narrow, full),
            first,
            size,
        )
        back_even = lax.ppermute(even_twin, "row", even)
        back_odd = lax.ppermute(odd_twin, "row", odd)
        whole = merged(
            band,
            [own_twin, back_even, back_odd],
            lambda own, other, odd_frame, has_odd: [True, True, has_odd],
        )
        from_twin.append(lax.ppermute(whole, "frame", twin))

    early_score = scored(
        band, queries, [keys, key_even], lambda own, other, odd_frame, has_odd: [True, own[2] >= 1]
    )
    late_score = scored(
        band,
        queries,
        [key_one, key_odd],
        lambda own, other, odd_frame, has_odd: [
            jnp.where(odd_frame, own[0], own[4]) >= 0,
            (own[2] >= 1) & has_odd,
        ],
    )
    near = neared(
        [early_score, late_score], [[(values,)], [(value_even,)], value_one, [(value_odd,)]]
    )
    far_score = scored(
        band,
        queries,
        [key_two],
        lambda own, other, odd_frame, has_odd: [jnp.where(odd_frame, own[4], own[0]) >= 0],
    )
    base, coef = based(far_score, near, from_twin)
    out = None
    for at, first in enumerate(ends[:-1]):
        out = finished(far_score[0], coef, value_two[at], base, out, first)
    return out


def solution(mesh):
    return jax.shard_map(
        per_device,
        mesh=mesh,
        in_specs=(
            P("frame", "row", None),
            P("frame", "row", None),
            P("frame", "row", None),
            P("frame", None),
        ),
        out_specs=P("frame", "row", None),
        check_vma=False,
    )
```

```python
import functools

import jax
import jax.numpy as jnp
from jax import lax
from jax.experimental import pallas as pl
from jax.experimental.pallas import tpu as pltpu
from jax.sharding import PartitionSpec as P


HEAD = 128
NEG = -1e30
RATE = HEAD ** (-0.5) * 1.4426950408889634
THIRD = 32
BATCH = 5
VMEM = pl.BlockSpec(memory_space=pltpu.VMEM)
SMEM = pl.BlockSpec(memory_space=pltpu.SMEM)
HBM = pl.BlockSpec(memory_space=pltpu.HBM)
GRANT = pltpu.CompilerParams(vmem_limit_bytes=16 << 20)


def column(index):
    return slice(index * HEAD, (index + 1) * HEAD)


def raw_scores(key, query):
    return lax.dot_general(
        key, query, (((1,), (1,)), ((), ())), preferred_element_type=jnp.float32
    )


def weighted(value, weights):
    return lax.dot_general(
        value, weights, (((0,), (0,)), ((), ())), preferred_element_type=jnp.float32
    )


def softmax_rows(raw):
    largest = functools.reduce(
        jnp.maximum, [jnp.max(part, axis=0, keepdims=True) for part in raw]
    )
    expos = [jnp.exp2((part - largest) * RATE) for part in raw]
    total = sum(jnp.sum(expo, axis=0, keepdims=True) for expo in expos)
    return [expo.astype(jnp.bfloat16) for expo in expos], total, largest


def thirds(value):
    high = value.astype(jnp.bfloat16).astype(jnp.float32)
    middle = (value - high).astype(jnp.bfloat16).astype(jnp.float32)
    return high, middle, value - high - middle


def packed(value):
    lane = lax.broadcasted_iota(jnp.int32, value.shape, 1)
    high, middle, low = thirds(value)
    rest = jnp.where(
        lane < 2 * THIRD, pltpu.roll(middle, THIRD, 1), pltpu.roll(low, 2 * THIRD, 1)
    )
    return jnp.where(lane < THIRD, high, rest).astype(jnp.bfloat16)


def read_log(block, heads):
    log = block[0, :, column(heads)].astype(jnp.float32)
    if block.dtype == jnp.float32:
        return log
    return log + pltpu.roll(log, HEAD - THIRD, 1) + pltpu.roll(log, HEAD - 2 * THIRD, 1)


def spread(table, n):
    row = lax.broadcasted_iota(jnp.int32, (HEAD, HEAD), 0)
    chosen = (row == n) | (row == THIRD + n) | (row == 2 * THIRD + n)
    return jnp.dot(
        table,
        jnp.where(chosen, 1.0, 0.0).astype(jnp.bfloat16),
        preferred_element_type=jnp.float32,
    )


def shares(logs):
    largest = functools.reduce(jnp.maximum, logs)
    expos = [jnp.exp2(log - largest) for log in logs]
    total = sum(expos)
    inverse = 1.0 / total
    return [expo * inverse for expo in expos], largest + jnp.log2(total)


def kept(rule, band_ref, twin_ref):
    odd_frame = lax.axis_index("frame") % 2 == 1
    row = lax.axis_index("row")
    return rule(
        [band_ref[0, i] for i in range(5)],
        [twin_ref[0, i] for i in range(5)] if twin_ref is not None else None,
        odd_frame,
        (row > 0) & (row < lax.axis_size("row") - 1),
    )


def grouped(refs, sizes):
    groups, at = [], 0
    for size in sizes:
        groups.append(refs[at : at + size])
        at += size
    return groups


def parts_kernel(query_count, key_count, shares_of, first, heads, rule, *refs):
    band_ref, twin_ref, refs = refs[0], refs[1], refs[2:]
    queries = refs[:query_count]
    keys = refs[query_count : query_count + key_count]
    values = grouped(refs[query_count + key_count : query_count + key_count + sum(shares_of)], shares_of)
    outs = refs[query_count + key_count + sum(shares_of) : -1]
    log_scratch = refs[-1]
    rows = queries[0].shape[1]
    wide = query_count * rows
    lane = lax.broadcasted_iota(jnp.int32, (1, wide), 1)
    keeps = kept(rule, band_ref, twin_ref)
    biases = []
    for i in range(key_count):
        bias = jnp.zeros((1, wide), jnp.float32)
        for at in range(query_count):
            if keeps[at][i] is not True:
                bias = jnp.where(
                    (lane >= at * rows) & (lane < (at + 1) * rows),
                    jnp.where(keeps[at][i], 0.0, NEG),
                    bias,
                )
        biases.append(bias)
    log_scratch[...] = jnp.zeros(log_scratch.shape, jnp.float32)

    def of(ref, n):
        start = 0 if ref.shape[2] == heads * HEAD else first
        return ref[0, :, column(start + n)]

    def score(n):
        query = jnp.concatenate([of(ref, n) for ref in queries], 0)
        return [raw_scores(of(key, n), query) + bias for key, bias in zip(keys, biases)]

    def attend(n, weights, total, largest):
        summed = sum(
            weighted(sum(of(ref, n) for ref in value), part)
            for value, part in zip(values, weights)
        )
        log_scratch[n : n + 1, :] = largest * RATE + jnp.log2(total)
        normed = (summed * (1.0 / total)).T
        for at, out in enumerate(outs):
            out[0, :, column(n)] = normed[at * rows : (at + 1) * rows].astype(out.dtype)

    raw = score(0)
    before = None
    for n in range(heads):
        later = score(n + 1) if n + 1 < heads else None
        now = softmax_rows(raw)
        if before is not None:
            attend(n - 1, *before)
        before, raw = now, later
    attend(heads - 1, *before)
    logs = log_scratch[...].T
    for at, out in enumerate(outs):
        log = logs[at * rows : (at + 1) * rows]
        out[0, :, column(heads)] = log if out.dtype == jnp.float32 else packed(log)


def parts(bands, queries, keys, values, rule, kinds, first, heads):
    rows = queries[0].shape[1]
    wide = len(queries) * rows
    blocks = len(queries) * len(keys)
    width = heads * HEAD
    shares_of = tuple(len(value) for value in values)
    flat = [piece for value in values for piece in value]
    return pl.pallas_call(
        functools.partial(
            parts_kernel, len(queries), len(keys), shares_of, first, heads, rule
        ),
        in_specs=[SMEM] * 2 + [VMEM] * (len(queries) + len(keys) + len(flat)),
        out_specs=[VMEM] * len(queries),
        out_shape=[
            jax.ShapeDtypeStruct((1, rows, width + HEAD), kind) for kind in kinds
        ],
        scratch_shapes=[pltpu.VMEM((HEAD, wide), jnp.float32)],
        compiler_params=GRANT,
        cost_estimate=pl.CostEstimate(
            flops=4 * rows * rows * width * blocks,
            bytes_accessed=2 * rows * width * (2 * len(queries) + 2 * len(keys)),
            transcendentals=rows * rows * heads * blocks,
        ),
    )(*bands, *queries, *keys, *flat)


def merge_kernel(heads, rule, band_ref, *refs):
    blocks, out_ref = refs[:-1], refs[-1]
    keeps = kept(rule, band_ref, None)
    logs = []
    for keep, block in zip(keeps, blocks):
        log = read_log(block, heads)
        logs.append(log if keep is True else jnp.where(keep, log, NEG))
    weights, log = shares(logs)
    tables = [packed(weight) for weight in weights]
    for n in range(heads):
        cols = column(n)
        out_ref[0, :, cols] = sum(
            spread(table, n) * block[0, :, cols].astype(jnp.float32)
            for table, block in zip(tables, blocks)
        ).astype(out_ref.dtype)
    out_ref[0, :, column(heads)] = packed(log)


def merged(band, blocks, rule):
    rows, width = blocks[0].shape[1:]
    heads = width // HEAD - 1
    return pl.pallas_call(
        functools.partial(merge_kernel, heads, rule),
        in_specs=[SMEM] + [VMEM] * len(blocks),
        out_specs=VMEM,
        out_shape=jax.ShapeDtypeStruct((1, rows, width), jnp.bfloat16),
        compiler_params=GRANT,
        cost_estimate=pl.CostEstimate(
            flops=2 * rows * width * len(blocks),
            bytes_accessed=2 * rows * width * (len(blocks) + 1),
            transcendentals=0,
        ),
    )(band, *blocks)


def score_kernel(heads, rule, band_ref, query_ref, *refs):
    keys, (weight_ref, table_ref, scratch) = refs[:-3], refs[-3:]
    biases = [
        None if keep is True else jnp.where(keep, 0.0, NEG)
        for keep in kept(rule, band_ref, None)
    ]
    scratch[...] = jnp.zeros(scratch.shape, jnp.float32)

    def score(n):
        cols = column(n)
        parts = [raw_scores(key[0, :, cols], query_ref[0, :, cols]) for key in keys]
        return [part if bias is None else part + bias for part, bias in zip(parts, biases)]

    raw = score(0)
    for n in range(heads):
        later = score(n + 1) if n + 1 < heads else None
        weights, total, largest = softmax_rows(raw)
        for at, weight in enumerate(weights):
            weight_ref[at, n] = weight.T
        scratch[0, n : n + 1, :] = largest * RATE + jnp.log2(total)
        scratch[1, n : n + 1, :] = 1.0 / total
        raw = later
    table_ref[0] = scratch[0].T
    table_ref[1] = scratch[1].T


def scored(band, query, keys, rule):
    rows, width = query.shape[1:]
    heads = width // HEAD
    return pl.pallas_call(
        functools.partial(score_kernel, heads, rule),
        in_specs=[SMEM] + [VMEM] * (1 + len(keys)),
        out_specs=[VMEM] * 2,
        out_shape=[
            jax.ShapeDtypeStruct((len(keys), heads, rows, rows), jnp.bfloat16),
            jax.ShapeDtypeStruct((2, rows, HEAD), jnp.float32),
        ],
        scratch_shapes=[pltpu.VMEM((2, HEAD, rows), jnp.float32)],
        compiler_params=GRANT,
        cost_estimate=pl.CostEstimate(
            flops=2 * rows * rows * width * len(keys),
            bytes_accessed=6 * rows * width,
            transcendentals=rows * rows * heads * len(keys),
        ),
    )(band, query, *keys)


def near_kernel(counts, shares_of, sources, heads, *refs):
    size = len(counts)
    weight_refs, table_refs = refs[:size], refs[size : 2 * size]
    pieces, out_ref = grouped(refs[2 * size : -1], shares_of), refs[-1]
    portions, log = shares([table_ref[0] for table_ref in table_refs])
    tables = [
        packed(portion * table_ref[1]) for portion, table_ref in zip(portions, table_refs)
    ]
    for n in range(heads):
        out = 0.0
        at = 0
        for count, weight_ref, table in zip(counts, weight_refs, tables):
            summed = 0.0
            for i in range(count):
                piece, index = sources[at][n]
                value = sum(ref[0, :, column(index)] for ref in pieces[piece])
                summed = summed + jnp.dot(
                    weight_ref[i, n], value, preferred_element_type=jnp.float32
                )
                at += 1
            out = out + summed * spread(table, n)
        out_ref[0, :, column(n)] = out
    out_ref[0, :, column(heads)] = log


def neared(scores, values):
    heads, rows = scores[0][0].shape[1:3]
    counts = tuple(weights.shape[0] for weights, _ in scores)
    sources, pieces = [], []
    for value in values:
        source = []
        for piece in value:
            size = piece[0].shape[2] // HEAD
            source += [(len(pieces), n) for n in range(size)]
            pieces.append(piece)
        sources.append(tuple(source))
    flat = [ref for piece in pieces for ref in piece]
    width = heads * HEAD
    return pl.pallas_call(
        functools.partial(
            near_kernel,
            counts,
            tuple(len(piece) for piece in pieces),
            tuple(sources),
            heads,
        ),
        in_specs=[VMEM] * (2 * len(scores) + len(flat)),
        out_specs=VMEM,
        out_shape=jax.ShapeDtypeStruct((1, rows, width + HEAD), jnp.float32),
        compiler_params=GRANT,
        cost_estimate=pl.CostEstimate(
            flops=2 * rows * rows * width * len(values),
            bytes_accessed=2 * rows * width * (len(values) + 4),
            transcendentals=0,
        ),
    )(*[score[0] for score in scores], *[score[1] for score in scores], *flat)


def base_kernel(sizes, heads, table_ref, near_ref, *refs):
    pieces, (out_ref, coef_ref) = refs[: len(sizes)], refs[len(sizes) :]
    lane = lax.broadcasted_iota(jnp.int32, (out_ref.shape[1], HEAD), 1)
    log, place = None, []
    for at, (piece, size) in enumerate(zip(pieces, sizes)):
        part = read_log(piece, size)
        if at:
            part = jnp.where(lane >= len(place), pltpu.roll(part, len(place), 1), log)
        log = part
        place += [(at, n) for n in range(size)]
    weights, _ = shares([table_ref[0], read_log(near_ref, heads), log])
    coef_ref[...] = packed(weights[0] * table_ref[1])
    near_table, twin_table = packed(weights[1]), packed(weights[2])
    for n in range(heads):
        piece, index = place[n]
        block = pieces[piece][0, :, column(index)].astype(jnp.float32)
        out_ref[0, :, column(n)] = (
            spread(near_table, n) * near_ref[0, :, column(n)] + spread(twin_table, n) * block
        )


def based(score, near, pieces):
    table = score[1]
    rows = near.shape[1]
    heads = near.shape[2] // HEAD - 1
    sizes = tuple(piece.shape[2] // HEAD - 1 for piece in pieces)
    return pl.pallas_call(
        functools.partial(base_kernel, sizes, heads),
        in_specs=[VMEM] * (2 + len(pieces)),
        out_specs=[VMEM, VMEM],
        out_shape=[
            jax.ShapeDtypeStruct((1, rows, heads * HEAD), jnp.float32),
            jax.ShapeDtypeStruct((rows, HEAD), jnp.bfloat16),
        ],
        compiler_params=GRANT,
        cost_estimate=pl.CostEstimate(
            flops=4 * rows * heads * HEAD,
            bytes_accessed=12 * rows * heads * HEAD,
            transcendentals=0,
        ),
    )(table, near, *pieces)


def final_kernel(first, heads, weight_ref, coef_ref, value_ref, base_ref, *refs):
    out_ref, scratch, sems = refs[-3:]
    copies = []
    for n in range(heads):
        cols = column(first + n)
        summed = jnp.dot(
            weight_ref[0, first + n],
            value_ref[0, :, column(n)],
            preferred_element_type=jnp.float32,
        )
        out = summed * spread(coef_ref[...], first + n) + base_ref[0, :, cols]
        scratch[:, column(n)] = out.astype(scratch.dtype)
        if (n + 1) % BATCH == 0 or n + 1 == heads:
            start = n // BATCH * BATCH
            done = slice(start * HEAD, (n + 1) * HEAD)
            target = slice((first + start) * HEAD, (first + n + 1) * HEAD)
            copy = pltpu.make_async_copy(
                scratch.at[:, done], out_ref.at[0, :, target], sems.at[n // BATCH]
            )
            copy.start()
            copies.append(copy)
    for copy in copies:
        copy.wait()


def finished(weights, coef, value, base, whole, first):
    rows, width = base.shape[1:]
    heads = value.shape[2] // HEAD
    return pl.pallas_call(
        functools.partial(final_kernel, first, heads),
        in_specs=[VMEM] * 4 + [HBM] * (whole is not None),
        out_specs=HBM,
        out_shape=jax.ShapeDtypeStruct((1, rows, width), value.dtype),
        scratch_shapes=[
            pltpu.VMEM((rows, heads * HEAD), value.dtype),
            pltpu.SemaphoreType.DMA((-(-heads // BATCH),)),
        ],
        input_output_aliases={4: 0} if whole is not None else {},
        compiler_params=GRANT,
        cost_estimate=pl.CostEstimate(
            flops=2 * rows * rows * heads * HEAD,
            bytes_accessed=8 * rows * heads * HEAD,
            transcendentals=0,
        ),
    )(weights, coef, value, base, *([] if whole is None else [whole]))


def per_device(queries, keys, values, band):
    frames, bands = lax.axis_size("frame"), lax.axis_size("row")
    toward = [(f, (f + 2) % frames) if f % 2 else (f, (f - 2) % frames) for f in range(frames)]
    away = [(target, source) for source, target in toward]
    twin = [(f, f ^ 1) for f in range(frames)]
    even = [(r, r ^ 1) for r in range(bands)]
    odd = [(r, r + 1) for r in range(1, bands - 1, 2)]
    odd += [(target, source) for source, target in odd]

    narrow, full = jnp.bfloat16, jnp.float32
    heads = queries.shape[2] // HEAD
    half = heads // 2
    spans = [(0, half), (half, heads - half)]

    cuts = [slice(first * HEAD, (first + size) * HEAD) for first, size in spans]
    value_halves = [values[:, :, cut] for cut in cuts]
    ends = [0, heads - heads // 5, heads]
    value_parts = [
        values[:, :, start * HEAD : stop * HEAD] for start, stop in zip(ends, ends[1:])
    ]
    beyond = [(a, b) for a, b in toward if abs(a - b) != 2]
    within = [(a, b) for a, b in toward if abs(a - b) == 2]

    key_one = lax.ppermute(keys, "frame", toward)
    value_one = [
        (lax.ppermute(value_halves[0], "frame", toward),),
        (
            lax.ppermute(value_halves[1], "frame", within),
            lax.ppermute(value_halves[1], "frame", beyond),
        ),
    ]
    key_two = lax.ppermute(keys, "frame", away)
    value_two = [lax.ppermute(piece, "frame", away) for piece in value_parts]
    query_twin = []
    for cut in cuts:
        query_twin.append(lax.ppermute(queries[:, :, cut], "frame", twin))
    band_twin = lax.ppermute(band, "frame", twin)
    key_even = lax.ppermute(keys, "row", even)
    key_odd = lax.ppermute(keys, "row", odd)
    value_even = lax.ppermute(values, "row", even)
    value_odd = lax.ppermute(values, "row", odd)
    twin_even = [lax.ppermute(query_twin[span], "row", even) for span in (0, 1)]
    twin_odd = [lax.ppermute(query_twin[span], "row", odd) for span in (0, 1)]

    def twin_rule(own, other, odd_frame, has_odd):
        here = jnp.where(odd_frame, other[3], other[1])
        there = jnp.where(odd_frame, other[1], other[3])
        beside = [here >= 1, there >= 1]
        return [beside, beside, [here >= 0, there >= 0]]

    from_twin = []
    for span, (first, size) in enumerate(spans):
        even_twin, odd_twin, own_twin = parts(
            (band, band_twin),
            [twin_even[span], twin_odd[span], query_twin[span]],
            [keys, key_one],
            [(values,), value_one[span]],
            twin_rule,
            (full, narrow, full),
            first,
            size,
        )
        back_even = lax.ppermute(even_twin, "row", even)
        back_odd = lax.ppermute(odd_twin, "row", odd)
        whole = merged(
            band,
            [own_twin, back_even, back_odd],
            lambda own, other, odd_frame, has_odd: [True, True, has_odd],
        )
        from_twin.append(lax.ppermute(whole, "frame", twin))

    early_score = scored(
        band,
        queries,
        [keys, key_even],
        lambda own, other, odd_frame, has_odd: [True, own[2] >= 1],
    )
    late_score = scored(
        band,
        queries,
        [key_one, key_odd],
        lambda own, other, odd_frame, has_odd: [
            jnp.where(odd_frame, own[0], own[4]) >= 0,
            (own[2] >= 1) & has_odd,
        ],
    )
    near = neared(
        [early_score, late_score],
        [[(values,)], [(value_even,)], value_one, [(value_odd,)]],
    )
    far_score = scored(
        band,
        queries,
        [key_two],
        lambda own, other, odd_frame, has_odd: [jnp.where(odd_frame, own[4], own[0]) >= 0],
    )
    base, coef = based(far_score, near, from_twin)
    out = None
    for at, first in enumerate(ends[:-1]):
        out = finished(far_score[0], coef, value_two[at], base, out, first)
    return out


def solution(mesh):
    return jax.shard_map(
        per_device,
        mesh=mesh,
        in_specs=(
            P("frame", "row", None),
            P("frame", "row", None),
            P("frame", "row", None),
            P("frame", None),
        ),
        out_specs=P("frame", "row", None),
        check_vma=False,
    )
```

```python
import functools

import jax
import jax.numpy as jnp
from jax import lax
from jax.experimental import pallas as pl
from jax.experimental.pallas import tpu as pltpu
from jax.sharding import PartitionSpec as P


HEAD = 128
NEG = -1e30
RATE = HEAD ** (-0.5) * 1.4426950408889634
THIRD = 32
BATCH = 5
VMEM = pl.BlockSpec(memory_space=pltpu.VMEM)
SMEM = pl.BlockSpec(memory_space=pltpu.SMEM)
HBM = pl.BlockSpec(memory_space=pltpu.HBM)
GRANT = pltpu.CompilerParams(vmem_limit_bytes=16 << 20)


def column(index):
    return slice(index * HEAD, (index + 1) * HEAD)


def raw_scores(key, query):
    return lax.dot_general(
        key, query, (((1,), (1,)), ((), ())), preferred_element_type=jnp.float32
    )


def weighted(value, weights):
    return lax.dot_general(
        value, weights, (((0,), (0,)), ((), ())), preferred_element_type=jnp.float32
    )


def softmax_rows(raw):
    largest = functools.reduce(
        jnp.maximum, [jnp.max(part, axis=0, keepdims=True) for part in raw]
    )
    expos = [jnp.exp2((part - largest) * RATE) for part in raw]
    total = sum(jnp.sum(expo, axis=0, keepdims=True) for expo in expos)
    return [expo.astype(jnp.bfloat16) for expo in expos], total, largest


def thirds(value):
    high = value.astype(jnp.bfloat16).astype(jnp.float32)
    middle = (value - high).astype(jnp.bfloat16).astype(jnp.float32)
    return high, middle, value - high - middle


def packed(value):
    lane = lax.broadcasted_iota(jnp.int32, value.shape, 1)
    high, middle, low = thirds(value)
    rest = jnp.where(
        lane < 2 * THIRD, pltpu.roll(middle, THIRD, 1), pltpu.roll(low, 2 * THIRD, 1)
    )
    return jnp.where(lane < THIRD, high, rest).astype(jnp.bfloat16)


def read_log(block, heads):
    log = block[0, :, column(heads)].astype(jnp.float32)
    if block.dtype == jnp.float32:
        return log
    return log + pltpu.roll(log, HEAD - THIRD, 1) + pltpu.roll(log, HEAD - 2 * THIRD, 1)


def spread(table, n):
    row = lax.broadcasted_iota(jnp.int32, (HEAD, HEAD), 0)
    chosen = (row == n) | (row == THIRD + n) | (row == 2 * THIRD + n)
    return jnp.dot(
        table,
        jnp.where(chosen, 1.0, 0.0).astype(jnp.bfloat16),
        preferred_element_type=jnp.float32,
    )


def shares(logs):
    largest = functools.reduce(jnp.maximum, logs)
    expos = [jnp.exp2(log - largest) for log in logs]
    total = sum(expos)
    inverse = 1.0 / total
    return [expo * inverse for expo in expos], largest + jnp.log2(total)


def kept(rule, band_ref, twin_ref):
    odd_frame = lax.axis_index("frame") % 2 == 1
    row = lax.axis_index("row")
    return rule(
        [band_ref[0, i] for i in range(5)],
        [twin_ref[0, i] for i in range(5)] if twin_ref is not None else None,
        odd_frame,
        (row > 0) & (row < lax.axis_size("row") - 1),
    )


def grouped(refs, sizes):
    groups, at = [], 0
    for size in sizes:
        groups.append(refs[at : at + size])
        at += size
    return groups


def parts_kernel(query_count, key_count, shares_of, first, heads, rule, *refs):
    band_ref, twin_ref, refs = refs[0], refs[1], refs[2:]
    queries = refs[:query_count]
    keys = refs[query_count : query_count + key_count]
    values = grouped(refs[query_count + key_count : query_count + key_count + sum(shares_of)], shares_of)
    outs = refs[query_count + key_count + sum(shares_of) : -1]
    log_scratch = refs[-1]
    rows = queries[0].shape[1]
    wide = query_count * rows
    lane = lax.broadcasted_iota(jnp.int32, (1, wide), 1)
    keeps = kept(rule, band_ref, twin_ref)
    biases = []
    for i in range(key_count):
        bias = jnp.zeros((1, wide), jnp.float32)
        for at in range(query_count):
            if keeps[at][i] is not True:
                bias = jnp.where(
                    (lane >= at * rows) & (lane < (at + 1) * rows),
                    jnp.where(keeps[at][i], 0.0, NEG),
                    bias,
                )
        biases.append(bias)
    log_scratch[...] = jnp.zeros(log_scratch.shape, jnp.float32)

    def of(ref, n):
        start = 0 if ref.shape[2] == heads * HEAD else first
        return ref[0, :, column(start + n)]

    def score(n):
        query = jnp.concatenate([of(ref, n) for ref in queries], 0)
        return [raw_scores(of(key, n), query) + bias for key, bias in zip(keys, biases)]

    def attend(n, weights, total, largest):
        summed = sum(
            weighted(sum(of(ref, n) for ref in value), part)
            for value, part in zip(values, weights)
        )
        log_scratch[n : n + 1, :] = largest * RATE + jnp.log2(total)
        normed = (summed * (1.0 / total)).T
        for at, out in enumerate(outs):
            out[0, :, column(n)] = normed[at * rows : (at + 1) * rows].astype(out.dtype)

    raw = score(0)
    before = None
    for n in range(heads):
        later = score(n + 1) if n + 1 < heads else None
        now = softmax_rows(raw)
        if before is not None:
            attend(n - 1, *before)
        before, raw = now, later
    attend(heads - 1, *before)
    logs = log_scratch[...].T
    for at, out in enumerate(outs):
        log = logs[at * rows : (at + 1) * rows]
        out[0, :, column(heads)] = log if out.dtype == jnp.float32 else packed(log)


def parts(bands, queries, keys, values, rule, kinds, first, heads):
    rows = queries[0].shape[1]
    wide = len(queries) * rows
    blocks = len(queries) * len(keys)
    width = heads * HEAD
    shares_of = tuple(len(value) for value in values)
    flat = [piece for value in values for piece in value]
    return pl.pallas_call(
        functools.partial(
            parts_kernel, len(queries), len(keys), shares_of, first, heads, rule
        ),
        in_specs=[SMEM] * 2 + [VMEM] * (len(queries) + len(keys) + len(flat)),
        out_specs=[VMEM] * len(queries),
        out_shape=[
            jax.ShapeDtypeStruct((1, rows, width + HEAD), kind) for kind in kinds
        ],
        scratch_shapes=[pltpu.VMEM((HEAD, wide), jnp.float32)],
        compiler_params=GRANT,
        cost_estimate=pl.CostEstimate(
            flops=4 * rows * rows * width * blocks,
            bytes_accessed=2 * rows * width * (2 * len(queries) + 2 * len(keys)),
            transcendentals=rows * rows * heads * blocks,
        ),
    )(*bands, *queries, *keys, *flat)


def merge_kernel(heads, rule, first, band_ref, *refs):
    if first:
        earlier_ref, blocks, out_ref = refs[0], refs[1:-1], refs[-1]
    else:
        blocks, (out_ref, log_ref) = refs[:-2], refs[-2:]
    keeps = kept(rule, band_ref, None)
    logs = []
    for keep, block in zip(keeps, blocks):
        log = read_log(block, heads)
        logs.append(log if keep is True else jnp.where(keep, log, NEG))
    weights, log = shares(logs)
    tables = [packed(weight) for weight in weights]
    for n in range(heads):
        cols = column(n)
        out_ref[0, :, cols] = sum(
            spread(table, n) * block[0, :, cols].astype(jnp.float32)
            for table, block in zip(tables, blocks)
        ).astype(out_ref.dtype)
    if first:
        lane = lax.broadcasted_iota(jnp.int32, log.shape, 1)
        log = jnp.where(lane < first, earlier_ref[...], pltpu.roll(log, first, 1))
        out_ref[0, :, column(heads)] = packed(log)
    else:
        log_ref[...] = log


def merged(band, blocks, rule, earlier, first):
    rows, width = blocks[0].shape[1:]
    heads = width // HEAD - 1
    extra = [] if earlier is None else [earlier]
    out_shape = [
        jax.ShapeDtypeStruct((1, rows, width - (0 if extra else HEAD)), jnp.bfloat16)
    ]
    if not extra:
        out_shape.append(jax.ShapeDtypeStruct((rows, HEAD), jnp.float32))
    return pl.pallas_call(
        functools.partial(merge_kernel, heads, rule, first),
        in_specs=[SMEM] + [VMEM] * (len(extra) + len(blocks)),
        out_specs=[VMEM] * len(out_shape),
        out_shape=out_shape,
        compiler_params=GRANT,
        cost_estimate=pl.CostEstimate(
            flops=2 * rows * width * len(blocks),
            bytes_accessed=2 * rows * width * (len(blocks) + 1),
            transcendentals=0,
        ),
    )(band, *extra, *blocks)


def score_kernel(heads, rule, band_ref, query_ref, *refs):
    keys, (weight_ref, table_ref, scratch) = refs[:-3], refs[-3:]
    biases = [
        None if keep is True else jnp.where(keep, 0.0, NEG)
        for keep in kept(rule, band_ref, None)
    ]
    scratch[...] = jnp.zeros(scratch.shape, jnp.float32)

    def score(n):
        cols = column(n)
        parts = [raw_scores(key[0, :, cols], query_ref[0, :, cols]) for key in keys]
        return [part if bias is None else part + bias for part, bias in zip(parts, biases)]

    raw = score(0)
    for n in range(heads):
        later = score(n + 1) if n + 1 < heads else None
        weights, total, largest = softmax_rows(raw)
        for at, weight in enumerate(weights):
            weight_ref[at, n] = weight.T
        scratch[0, n : n + 1, :] = largest * RATE + jnp.log2(total)
        scratch[1, n : n + 1, :] = 1.0 / total
        raw = later
    table_ref[0] = scratch[0].T
    table_ref[1] = scratch[1].T


def scored(band, query, keys, rule):
    rows, width = query.shape[1:]
    heads = width // HEAD
    return pl.pallas_call(
        functools.partial(score_kernel, heads, rule),
        in_specs=[SMEM] + [VMEM] * (1 + len(keys)),
        out_specs=[VMEM] * 2,
        out_shape=[
            jax.ShapeDtypeStruct((len(keys), heads, rows, rows), jnp.bfloat16),
            jax.ShapeDtypeStruct((2, rows, HEAD), jnp.float32),
        ],
        scratch_shapes=[pltpu.VMEM((2, HEAD, rows), jnp.float32)],
        compiler_params=GRANT,
        cost_estimate=pl.CostEstimate(
            flops=2 * rows * rows * width * len(keys),
            bytes_accessed=6 * rows * width,
            transcendentals=rows * rows * heads * len(keys),
        ),
    )(band, query, *keys)


def near_kernel(counts, shares_of, sources, heads, *refs):
    size = len(counts)
    weight_refs, table_refs = refs[:size], refs[size : 2 * size]
    pieces, out_ref = grouped(refs[2 * size : -1], shares_of), refs[-1]
    portions, log = shares([table_ref[0] for table_ref in table_refs])
    tables = [
        packed(portion * table_ref[1]) for portion, table_ref in zip(portions, table_refs)
    ]
    for n in range(heads):
        out = 0.0
        at = 0
        for count, weight_ref, table in zip(counts, weight_refs, tables):
            summed = 0.0
            for i in range(count):
                piece, index = sources[at][n]
                value = sum(ref[0, :, column(index)] for ref in pieces[piece])
                summed = summed + jnp.dot(
                    weight_ref[i, n], value, preferred_element_type=jnp.float32
                )
                at += 1
            out = out + summed * spread(table, n)
        out_ref[0, :, column(n)] = out
    out_ref[0, :, column(heads)] = log


def neared(scores, values):
    heads, rows = scores[0][0].shape[1:3]
    counts = tuple(weights.shape[0] for weights, _ in scores)
    sources, pieces = [], []
    for value in values:
        source = []
        for piece in value:
            size = piece[0].shape[2] // HEAD
            source += [(len(pieces), n) for n in range(size)]
            pieces.append(piece)
        sources.append(tuple(source))
    flat = [ref for piece in pieces for ref in piece]
    width = heads * HEAD
    return pl.pallas_call(
        functools.partial(
            near_kernel,
            counts,
            tuple(len(piece) for piece in pieces),
            tuple(sources),
            heads,
        ),
        in_specs=[VMEM] * (2 * len(scores) + len(flat)),
        out_specs=VMEM,
        out_shape=jax.ShapeDtypeStruct((1, rows, width + HEAD), jnp.float32),
        compiler_params=GRANT,
        cost_estimate=pl.CostEstimate(
            flops=2 * rows * rows * width * len(values),
            bytes_accessed=2 * rows * width * (len(values) + 4),
            transcendentals=0,
        ),
    )(*[score[0] for score in scores], *[score[1] for score in scores], *flat)


def base_kernel(sizes, heads, table_ref, near_ref, *refs):
    pieces, (out_ref, coef_ref) = refs[: len(sizes)], refs[len(sizes) :]
    place = [(at, n) for at, size in enumerate(sizes) for n in range(size)]
    log = read_log(pieces[-1], sizes[-1])
    weights, _ = shares([table_ref[0], read_log(near_ref, heads), log])
    coef_ref[...] = packed(weights[0] * table_ref[1])
    near_table, twin_table = packed(weights[1]), packed(weights[2])
    for n in range(heads):
        piece, index = place[n]
        block = pieces[piece][0, :, column(index)].astype(jnp.float32)
        out_ref[0, :, column(n)] = (
            spread(near_table, n) * near_ref[0, :, column(n)] + spread(twin_table, n) * block
        )


def based(score, near, pieces):
    table = score[1]
    rows = near.shape[1]
    heads = near.shape[2] // HEAD - 1
    sizes = tuple(piece.shape[2] // HEAD for piece in pieces[:-1])
    sizes += (heads - sum(sizes),)
    return pl.pallas_call(
        functools.partial(base_kernel, sizes, heads),
        in_specs=[VMEM] * (2 + len(pieces)),
        out_specs=[VMEM, VMEM],
        out_shape=[
            jax.ShapeDtypeStruct((1, rows, heads * HEAD), jnp.float32),
            jax.ShapeDtypeStruct((rows, HEAD), jnp.bfloat16),
        ],
        compiler_params=GRANT,
        cost_estimate=pl.CostEstimate(
            flops=4 * rows * heads * HEAD,
            bytes_accessed=12 * rows * heads * HEAD,
            transcendentals=0,
        ),
    )(table, near, *pieces)


def final_kernel(first, heads, weight_ref, coef_ref, value_ref, base_ref, *refs):
    out_ref, scratch, sems = refs[-3:]
    copies = []
    for n in range(heads):
        cols = column(first + n)
        summed = jnp.dot(
            weight_ref[0, first + n],
            value_ref[0, :, column(n)],
            preferred_element_type=jnp.float32,
        )
        out = summed * spread(coef_ref[...], first + n) + base_ref[0, :, cols]
        scratch[:, column(n)] = out.astype(scratch.dtype)
        if (n + 1) % BATCH == 0 or n + 1 == heads:
            start = n // BATCH * BATCH
            done = slice(start * HEAD, (n + 1) * HEAD)
            target = slice((first + start) * HEAD, (first + n + 1) * HEAD)
            copy = pltpu.make_async_copy(
                scratch.at[:, done], out_ref.at[0, :, target], sems.at[n // BATCH]
            )
            copy.start()
            copies.append(copy)
    for copy in copies:
        copy.wait()


def finished(weights, coef, value, base, whole, first):
    rows, width = base.shape[1:]
    heads = value.shape[2] // HEAD
    return pl.pallas_call(
        functools.partial(final_kernel, first, heads),
        in_specs=[VMEM] * 4 + [HBM] * (whole is not None),
        out_specs=HBM,
        out_shape=jax.ShapeDtypeStruct((1, rows, width), value.dtype),
        scratch_shapes=[
            pltpu.VMEM((rows, heads * HEAD), value.dtype),
            pltpu.SemaphoreType.DMA((-(-heads // BATCH),)),
        ],
        input_output_aliases={4: 0} if whole is not None else {},
        compiler_params=GRANT,
        cost_estimate=pl.CostEstimate(
            flops=2 * rows * rows * heads * HEAD,
            bytes_accessed=8 * rows * heads * HEAD,
            transcendentals=0,
        ),
    )(weights, coef, value, base, *([] if whole is None else [whole]))


def per_device(queries, keys, values, band):
    frames, bands = lax.axis_size("frame"), lax.axis_size("row")
    toward = [(f, (f + 2) % frames) if f % 2 else (f, (f - 2) % frames) for f in range(frames)]
    away = [(target, source) for source, target in toward]
    twin = [(f, f ^ 1) for f in range(frames)]
    even = [(r, r ^ 1) for r in range(bands)]
    odd = [(r, r + 1) for r in range(1, bands - 1, 2)]
    odd += [(target, source) for source, target in odd]

    narrow, full = jnp.bfloat16, jnp.float32
    heads = queries.shape[2] // HEAD
    half = heads // 2
    spans = [(0, half), (half, heads - half)]

    cuts = [slice(first * HEAD, (first + size) * HEAD) for first, size in spans]
    value_halves = [values[:, :, cut] for cut in cuts]
    ends = [0, heads - heads // 5, heads]
    value_parts = [
        values[:, :, start * HEAD : stop * HEAD] for start, stop in zip(ends, ends[1:])
    ]
    beyond = [(a, b) for a, b in toward if abs(a - b) != 2]
    within = [(a, b) for a, b in toward if abs(a - b) == 2]

    key_one = lax.ppermute(keys, "frame", toward)
    value_one = [
        (lax.ppermute(value_halves[0], "frame", toward),),
        (
            lax.ppermute(value_halves[1], "frame", within),
            lax.ppermute(value_halves[1], "frame", beyond),
        ),
    ]
    key_two = lax.ppermute(keys, "frame", away)
    value_two = [lax.ppermute(piece, "frame", away) for piece in value_parts]
    query_twin = []
    for cut in cuts:
        query_twin.append(lax.ppermute(queries[:, :, cut], "frame", twin))
    band_twin = lax.ppermute(band, "frame", twin)
    key_even = lax.ppermute(keys, "row", even)
    key_odd = lax.ppermute(keys, "row", odd)
    value_even = lax.ppermute(values, "row", even)
    value_odd = lax.ppermute(values, "row", odd)
    twin_even = [lax.ppermute(query_twin[span], "row", even) for span in (0, 1)]
    twin_odd = [lax.ppermute(query_twin[span], "row", odd) for span in (0, 1)]

    def twin_rule(own, other, odd_frame, has_odd):
        here = jnp.where(odd_frame, other[3], other[1])
        there = jnp.where(odd_frame, other[1], other[3])
        beside = [here >= 1, there >= 1]
        return [beside, beside, [here >= 0, there >= 0]]

    from_twin = []
    merge_log = None
    for span, (first, size) in enumerate(spans):
        even_twin, odd_twin, own_twin = parts(
            (band, band_twin),
            [twin_even[span], twin_odd[span], query_twin[span]],
            [keys, key_one],
            [(values,), value_one[span]],
            twin_rule,
            (full, narrow, full),
            first,
            size,
        )
        back_even = lax.ppermute(even_twin, "row", even)
        back_odd = lax.ppermute(odd_twin, "row", odd)
        whole = merged(
            band,
            [own_twin, back_even, back_odd],
            lambda own, other, odd_frame, has_odd: [True, True, has_odd],
            merge_log,
            first,
        )
        merge_log = whole[-1]
        from_twin.append(lax.ppermute(whole[0], "frame", twin))

    early_score = scored(
        band,
        queries,
        [keys, key_even],
        lambda own, other, odd_frame, has_odd: [True, own[2] >= 1],
    )
    late_score = scored(
        band,
        queries,
        [key_one, key_odd],
        lambda own, other, odd_frame, has_odd: [
            jnp.where(odd_frame, own[0], own[4]) >= 0,
            (own[2] >= 1) & has_odd,
        ],
    )
    near = neared(
        [early_score, late_score],
        [[(values,)], [(value_even,)], value_one, [(value_odd,)]],
    )
    far_score = scored(
        band,
        queries,
        [key_two],
        lambda own, other, odd_frame, has_odd: [jnp.where(odd_frame, own[4], own[0]) >= 0],
    )
    base, coef = based(far_score, near, from_twin)
    out = None
    for at, first in enumerate(ends[:-1]):
        out = finished(far_score[0], coef, value_two[at], base, out, first)
    return out


def solution(mesh):
    return jax.shard_map(
        per_device,
        mesh=mesh,
        in_specs=(
            P("frame", "row", None),
            P("frame", "row", None),
            P("frame", "row", None),
            P("frame", None),
        ),
        out_specs=P("frame", "row", None),
        check_vma=False,
    )
```
